512 devices in a mesh: dp: 16 (over z), ctx: 32 (over x, y, core).
Axes of the slice: x: 4, y: 4, z: 16, core: 2. Of those that a mesh axis runs over, the one named last changes fastest.
Arguments:
- queries: bfloat16 [16, 4096, 2048], P('dp', 'ctx'), may hold values from -4.5 to 4.5
- key_rows: bfloat16 [16, 4096, 2048], P('dp', 'ctx'), may hold values from -4.5 to 4.5
- value_rows: bfloat16 [16, 4096, 2048], P('dp', 'ctx'), may hold values from -6 to 6
- doc_ids: int32 [16, 4096], P('dp', 'ctx'), may hold values from 0 to 7, never falling along the last dimension, each value on 1 to 1024 neighbouring positions
- gate_logit: float32 [16], replicated, may hold values from -2 to 2
- grad_out: bfloat16 [16, 4096, 2048], P('dp', 'ctx'), may hold values from -6 to 6
Outputs:
- attended: bfloat16 [16, 4096, 2048], P('dp', 'ctx')
- grad_queries: bfloat16 [16, 4096, 2048], P('dp', 'ctx')
- grad_keys: bfloat16 [16, 4096, 2048], P('dp', 'ctx')
- grad_values: bfloat16 [16, 4096, 2048], P('dp', 'ctx')
- grad_gate: float32 [16], replicated
The draws below stay inside these ranges and needn't reach their ends.
Inputs may be any that keep to these rules, and one draw needn't show every extreme that they name: `doc_ids`: within each stream ids start at 0, never fall and rise by one at each document start; all 8 documents occur, each of 1 to min(1024, 2048) tokens, one of exactly that many.
All inputs are finite; a program needn't handle non-finite values.
Results may differ from the reference program's by a relative error of at most 0.023.
Values may be sent and summed in bfloat16 or wider, within the bound.
A program may use at most 128 MiB of HBM per device.

```python
import math
import jax
import jax.numpy as jnp
import numpy as np
from jax import lax

HEADS = 16
HEAD_DIM = 128
SEG = 128
STREAMS = 16
LENGTH = 4096
DOCS = 8
N_CTX = 32


def drawn_pair(key):
    base_key = jax.random.fold_in(key, 7301)
    full_shape = (STREAMS, LENGTH, HEADS * HEAD_DIM)
    query_draw = jnp.clip(jax.random.normal(jax.random.fold_in(base_key, 1), full_shape, jnp.float32), -4.5, 4.5)
    key_draw = jnp.clip(jax.random.normal(jax.random.fold_in(base_key, 2), full_shape, jnp.float32), -4.5, 4.5)
    return (query_draw.astype(jnp.bfloat16), key_draw.astype(jnp.bfloat16))


def draw_queries(key, part):
    return drawn_pair(key)[0]


def draw_key_rows(key, part):
    return drawn_pair(key)[1]


def block_scale(stream_key, dims, split, smallest, high):
    factor_of, own = 1.0, jax.random.fold_in(stream_key, 6)
    for dim, shards_of in split:
        heights = jnp.exp(jax.random.uniform(jax.random.fold_in(own, dim), (shards_of,), jnp.float32, smallest / len(split), high / len(split)))
        factor_of = factor_of * jnp.repeat(heights, dims[dim] // shards_of).reshape([-1 if axis == dim else 1 for axis in range(len(dims))])
    return factor_of


def split_up(number_of, total, reach, slope):
    weights = [(1 << 20) // math.isqrt(rank ** slope) + 1 for rank in range(2, number_of + 1)]
    rest, counts = total - reach - (number_of - 1), [1] * (number_of - 1)
    while rest > 0:
        free = [i for i in range(number_of - 1) if counts[i] < reach]
        mass, remaining = sum([weights[i] for i in free]), rest
        for i in free:
            more = min(reach - counts[i], max(1, remaining * weights[i] // mass), rest)
            counts[i] = counts[i] + more
            rest = rest - more
    return np.array([reach] + counts)


def ragged(stream_key, number_of, total, limit, slope):
    if number_of == 2:
        one = jax.random.randint(stream_key, (), max(1, total - limit), min(limit, total - 1) + 1)
        return jnp.stack([one, total - one])
    sizes = jnp.asarray(split_up(number_of, total, limit, slope), jnp.int32)
    pairs = (number_of - 1) // 2
    source_of, taker = sizes[1:1 + 2 * pairs:2], sizes[2:2 + 2 * pairs:2]
    margin = jnp.minimum(source_of - 1, limit - taker)
    moved = jax.random.randint(jax.random.fold_in(stream_key, 1), (pairs,), 0, 1 << 20) % (margin + 1)
    sizes = sizes.at[1:1 + 2 * pairs:2].set(source_of - moved).at[2:2 + 2 * pairs:2].set(taker + moved)
    return sizes[jax.random.permutation(jax.random.fold_in(stream_key, 2), number_of)]


def noise(stream_key, shape, spread, limit, split=(), kind=jnp.bfloat16):
    values = spread * jax.random.normal(stream_key, shape, jnp.float32)
    if split:
        values = values * block_scale(stream_key, shape, split, -0.22, 0.18)
    return jnp.clip(values, -limit, limit).astype(kind)


def setup_inputs(seed: int = 0) -> dict:
    splits = jax.random.split(jax.random.key(seed), 7)
    queries = draw_queries(jax.random.fold_in(splits[6], 71), 0)
    key_rows = draw_key_rows(jax.random.fold_in(splits[6], 71), 0)
    value_rows = noise(splits[2], (STREAMS, LENGTH, HEADS * HEAD_DIM), 1.0, 6.0, ((0, 16), (1, 32)))
    doc_ids = jax.vmap(lambda own: jnp.searchsorted(jnp.cumsum(ragged(own, DOCS, LENGTH, min(8 * SEG, LENGTH // 2), 1)), jnp.arange(LENGTH), side="right"))(jax.random.split(splits[3], STREAMS)).reshape((STREAMS, LENGTH)).astype(jnp.int32)
    gate_logit = jnp.clip(jax.random.uniform(splits[4], (HEADS,), jnp.float32, -2.0, 2.0), -2.0, 2.0)
    grad_out = noise(splits[5], (STREAMS, LENGTH, HEADS * HEAD_DIM), 1.0, 6.0, ((0, 16), (1, 32)))
    return dict(queries=queries, key_rows=key_rows, value_rows=value_rows, doc_ids=doc_ids, gate_logit=gate_logit, grad_out=grad_out)


def feature(inputs):
    return jax.nn.elu(inputs) + 1.0

def tail_state(key_feat, value_feat, weight):
    lifted = feature(key_feat) * weight[:, None, None]
    memory = jnp.einsum('shd,she->hde', lifted, value_feat, precision=lax.Precision.HIGHEST)
    return (memory, lax.optimization_barrier(jnp.sum(lifted, axis=0)))

def retrieve(query_feat, memory, key_total, use_memory):
    lifted = feature(query_feat) * use_memory[:, None, None]
    numerator = jnp.einsum('thd,hde->the', lifted, memory, precision=lax.Precision.HIGHEST)
    denominator = jnp.maximum(jnp.einsum('thd,hd->th', lifted, key_total, precision=lax.Precision.HIGHEST), 1.0)
    return numerator / denominator[:, :, None]

def attend(query_rows, key_block, value_block, allowed):
    scaling = query_rows.shape[-1] ** (-0.5)
    scores = jnp.einsum('thd,shd->hts', query_rows.astype(jnp.float32), key_block.astype(jnp.float32)) * scaling
    scores = jnp.where(allowed[None], scores, -jnp.inf)
    row_top = lax.optimization_barrier(jnp.max(scores, axis=-1, keepdims=True))
    log_total = row_top + jnp.log(lax.optimization_barrier(jnp.sum(jnp.exp(scores - row_top), axis=-1, keepdims=True)))
    weights = jnp.exp(scores - log_total).astype(jnp.bfloat16)
    result = jnp.einsum('hts,shd->thd', weights.astype(jnp.float32), value_block.astype(jnp.float32))
    return (result, log_total[..., 0])

def attend_back(query_rows, key_block, value_block, allowed, log_total, grad_att, row_delta):
    scaling = query_rows.shape[-1] ** (-0.5)
    scores = jnp.einsum('thd,shd->hts', query_rows.astype(jnp.float32), key_block.astype(jnp.float32)) * scaling
    scores = jnp.where(allowed[None], scores, -jnp.inf)
    softmax = jnp.exp(scores - log_total[..., None])
    weights = softmax.astype(jnp.bfloat16)
    grad_weights = jnp.einsum('thd,shd->hts', grad_att.astype(jnp.float32), value_block.astype(jnp.float32))
    grad_scores = (softmax * (grad_weights - row_delta[..., None]) * scaling).astype(jnp.bfloat16)
    grad_query = jnp.einsum('hts,shd->thd', grad_scores.astype(jnp.float32), key_block.astype(jnp.float32))
    grad_key = jnp.einsum('hts,thd->shd', grad_scores.astype(jnp.float32), query_rows.astype(jnp.float32))
    grad_value = jnp.einsum('hts,thd->shd', weights.astype(jnp.float32), grad_att.astype(jnp.float32))
    return (grad_query, grad_key, grad_value)

def one_stream(queries, key_rows, value_rows, doc_ids, grad_out, gate):
    block_shape = (N_CTX, SEG, HEADS, HEAD_DIM)
    query_blk = queries.reshape(block_shape)
    key_blk = key_rows.reshape(block_shape)
    value_blk = value_rows.reshape(block_shape)
    id_blk = doc_ids.reshape(N_CTX, SEG)
    prior_keys = jnp.concatenate([jnp.zeros_like(key_blk[:1]), key_blk[:-1]], axis=0)
    prior_values = jnp.concatenate([jnp.zeros_like(value_blk[:1]), value_blk[:-1]], axis=0)
    prior_ids = jnp.concatenate([jnp.full((1, SEG), -1, jnp.int32), id_blk[:-1]], axis=0)
    window_keys = jnp.concatenate([prior_keys, key_blk], axis=1)
    window_values = jnp.concatenate([prior_values, value_blk], axis=1)
    window_ids = jnp.concatenate([prior_ids, id_blk], axis=1)
    row_pos = jnp.arange(SEG)[:, None]
    col_pos = jnp.arange(2 * SEG)[None, :]
    inside = (col_pos > row_pos) & (col_pos <= row_pos + SEG)
    allowed = inside[None] & (window_ids[:, None, :] == id_blk[:, :, None])
    local_out, log_total = jax.vmap(attend)(query_blk, window_keys, window_values, allowed)
    last_ids = id_blk[:, -1]
    prior_last = jnp.concatenate([jnp.full((1,), -1, jnp.int32), last_ids[:-1]])
    weight = (id_blk == last_ids[:, None]).astype(jnp.float32)
    resets = (last_ids != prior_last).astype(jnp.float32)
    use_memory = (id_blk == prior_last[:, None]).astype(jnp.float32)

    def all_tails(key_feat, value_feat):
        return jax.vmap(tail_state)(key_feat, value_feat, weight)
    (tail_mem, tail_total), tail_pull = jax.vjp(all_tails, key_blk.astype(jnp.float32), value_blk.astype(jnp.float32))

    def forward_step(carry, item):
        keep = 1.0 - item[2]
        return ((item[0] + keep * carry[0], item[1] + keep * carry[1]), (carry[0], carry[1]))
    zero_state = (jnp.zeros((HEADS, HEAD_DIM, HEAD_DIM), jnp.float32), jnp.zeros((HEADS, HEAD_DIM), jnp.float32))
    final_state, prefix = lax.scan(forward_step, zero_state, (tail_mem, tail_total, resets))

    def all_reads(query_feat, memory, key_total):
        return jax.vmap(retrieve)(query_feat, memory, key_total, use_memory)
    memory_out, read_pull = jax.vjp(all_reads, query_blk.astype(jnp.float32), prefix[0], prefix[1])
    gate_col = gate[:, None]
    mixed = gate_col * memory_out + (1.0 - gate_col) * local_out
    grad_mixed = grad_out.reshape(block_shape).astype(jnp.float32)
    grad_gate = lax.optimization_barrier(jnp.sum(grad_mixed * (memory_out - local_out), axis=(0, 1, 3))) * gate * (1.0 - gate)
    grad_att = ((1.0 - gate_col) * grad_mixed).astype(jnp.bfloat16)
    row_delta = jnp.swapaxes(lax.optimization_barrier(jnp.sum(grad_att.astype(jnp.float32) * local_out, axis=-1)), 1, 2)
    grad_query_local, grad_window_keys, grad_window_values = jax.vmap(attend_back)(query_blk, window_keys, window_values, allowed, log_total, grad_att, row_delta)
    from_next_keys = jnp.concatenate([grad_window_keys[1:, :SEG], jnp.zeros_like(grad_window_keys[:1, :SEG])], axis=0)
    from_next_values = jnp.concatenate([grad_window_values[1:, :SEG], jnp.zeros_like(grad_window_values[:1, :SEG])], axis=0)
    grad_query_mem, grad_prefix_mem, grad_prefix_total = read_pull(gate_col * grad_mixed)

    def backward_step(carry, item):
        keep = 1.0 - item[2]
        return ((item[0] + keep * carry[0], item[1] + keep * carry[1]), (carry[0], carry[1]))
    final_grad, carried = lax.scan(backward_step, zero_state, (grad_prefix_mem, grad_prefix_total, resets), reverse=True)
    grad_key_mem, grad_value_mem = tail_pull((carried[0], carried[1]))
    flat = (LENGTH, HEADS * HEAD_DIM)
    attended = mixed.astype(jnp.bfloat16).reshape(flat)
    grad_queries = (grad_query_local + grad_query_mem).astype(jnp.bfloat16).reshape(flat)
    grad_keys = (grad_window_keys[:, SEG:] + from_next_keys + grad_key_mem).astype(jnp.bfloat16).reshape(flat)
    grad_values = (grad_window_values[:, SEG:] + from_next_values + grad_value_mem).astype(jnp.bfloat16).reshape(flat)
    return (attended, grad_queries, grad_keys, grad_values, grad_gate)

def reference(queries, key_rows, value_rows, doc_ids, gate_logit, grad_out):
    gate = jax.nn.sigmoid(gate_logit)

    def per_stream(stream):
        return one_stream(stream[0], stream[1], stream[2], stream[3], stream[4], gate)
    results = lax.map(per_stream, (queries, key_rows, value_rows, doc_ids, grad_out))
    return (results[0], results[1], results[2], results[3], lax.optimization_barrier(jnp.sum(results[4], axis=0)))
```

```python
import functools
import math

import jax
import jax.numpy as jnp
from jax import lax
from jax.experimental import pallas as pl
from jax.experimental.pallas import tpu as pltpu
from jax.sharding import PartitionSpec as P

SEG = 128
DIM = 128
HEADS = 16
ROW = 8
REACH = 8
MESH = pl.DeviceIdType.MESH
F32 = jnp.float32
BF16 = jnp.bfloat16


def dot_nn(a, b):
    return lax.dot_general(a, b, (((1,), (0,)), ((), ())), preferred_element_type=F32)


def dot_nt(a, b):
    return lax.dot_general(a, b, (((1,), (1,)), ((), ())), preferred_element_type=F32)


def dot_tn(a, b):
    return lax.dot_general(a, b, (((0,), (0,)), ((), ())), preferred_element_type=F32)


def place_of(h):
    return lax.rem(lax.div(h, 2), 2) * 8 + lax.div(h, 4) * 2 + lax.rem(h, 2)


def columns(h):
    return pl.ds(pl.multiple_of(h * DIM, DIM), DIM)


def feature(x):
    return jnp.where(x > 0, x + 1.0, jnp.exp(jnp.minimum(x, 0.0)))


def kernel(
    n_ctx, n_dp,
    q_in, k_in, v_in, ids_in, gate_in, g_in,
    att_out, dq_out, dk_out, dv_out, gg_out,
    q_s, k_s, v_s, g_s, idr, kp, vp, fk, fq, den_s,
    fx, fxp, ftc, fta, fro, fri, fpo, fpc, fsx, fres,
    bx, bxp, btc, bta, bro, bri, bpo, bpc, bsx, bres,
    ol, dql, dkl, dvl, dks, dvs, dkn, dvn,
    att_o, dq_o, dk_o, dv_o,
    zt, zr, zb, dzt, dzr, cz, gt, gg, bias, wm, um,
    red_s, red_r,
    load_sem, out_sem, ids_ss, ids_rs, z_ss, z_rs, dz_ss, dz_rs,
    k_ss, k_rs, v_ss, v_rs, dk_ss, dk_rs, dv_ss, dv_rs,
    f_ss, f_rs, b_ss, b_rs, red_ss, red_rs,
):
    me = lax.axis_index("ctx")
    mz = lax.axis_index("dp")
    row = lax.div(me, ROW)
    spot = lax.rem(me, ROW)
    y = lax.div(spot, 2)
    core = lax.rem(me, 2)

    def at(offset):
        return {"ctx": lax.rem(me + offset + n_ctx, n_ctx)}

    def up(offset):
        return {"dp": lax.rem(mz + offset + n_dp, n_dp)}

    def remote(src, dst, ss, rs, device):
        return pltpu.make_async_remote_copy(
            src_ref=src, dst_ref=dst, send_sem=ss, recv_sem=rs,
            device_id=device, device_id_type=MESH,
        )

    loads = []
    for i, (src, dst) in enumerate(
        ((ids_in, idr.at[REACH]), (k_in, k_s), (v_in, v_s), (q_in, q_s), (g_in, g_s))
    ):
        copy = pltpu.make_async_copy(src, dst, load_sem.at[i])
        copy.start()
        loads.append(copy)
    barrier = pltpu.get_barrier_semaphore()
    near = [d for d in range(-REACH, REACH + 1) if d] + [n_ctx // 2]
    steps_z = []
    d = 1
    while d < n_dp:
        steps_z.append(d)
        d *= 2
    far = sorted({s % n_dp for d in steps_z for s in (d, -d)})
    for d in near:
        pl.semaphore_signal(barrier, inc=1, device_id=at(d), device_id_type=MESH)
    for d in far:
        pl.semaphore_signal(barrier, inc=1, device_id=up(d), device_id_type=MESH)

    for h in range(HEADS):
        logit = jnp.full((1, DIM), gate_in[0, h], F32)
        gt[h] = 1.0 / (1.0 + jnp.exp(-logit))
    loads[0].wait()
    own_ids = idr[REACH]
    own_cols = jnp.broadcast_to(own_ids.astype(F32), (SEG, SEG))
    own_rows = jnp.transpose(own_cols)
    own_last = own_ids[:, SEG - 1 :].astype(F32)
    wm[...] = (own_rows == own_last).astype(F32)
    loads[1].wait()
    loads[2].wait()
    pl.semaphore_wait(barrier, len(near) + len(far))

    id_sends = [d for d in range(-(REACH - 1), REACH + 1) if d]
    for i, d in enumerate(id_sends):
        remote(idr.at[REACH], idr.at[REACH - d], ids_ss.at[i], ids_rs.at[i], at(d)).start()

    def send_kv(h, carry):
        remote(k_s.at[:, columns(h)], kp.at[h], k_ss.at[h], k_rs.at[h], at(1)).start()
        remote(v_s.at[:, columns(h)], vp.at[h], v_ss.at[h], v_rs.at[h], at(1)).start()
        return carry

    lax.fori_loop(0, HEADS, send_kv, 0)

    def tails(h, carry):
        lifted = feature(k_s[:, columns(h)].astype(F32)) * wm[...]
        short = lifted.astype(BF16)
        fk[h] = short
        zt[h] = jnp.sum(lifted, axis=0, keepdims=True)
        fx[place_of(h)] = dot_tn(short, v_s[:, columns(h)]).astype(BF16)
        return carry

    lax.fori_loop(0, HEADS, tails, 0, unroll=2)

    def pair_send(x, xp, ss, rs):
        other = pl.ds(pl.multiple_of((1 - core) * 8, 8), 8)
        return remote(x.at[other], xp, ss.at[0], rs.at[0], at(1 - 2 * core))

    f_pair = pair_send(fx, fxp, f_ss, f_rs)
    f_pair.start()
    for d in range(1, REACH + 1):
        remote(zt, zr.at[d - 1], z_ss.at[d - 1], z_rs.at[d - 1], at(d)).start()

    for i, d in enumerate(id_sends):
        remote(idr.at[REACH], idr.at[REACH - d], ids_ss.at[i], ids_rs.at[i], at(d)).wait()

    def last(offset):
        return idr[REACH + offset][:, SEG - 1 :]

    def same(a, b):
        return (last(a) == last(b)).astype(F32)

    is_late = core.astype(F32)
    is_early = 1.0 - is_late
    not_first = (me > 0).astype(F32)
    first_chip = (row > 0).astype(F32)
    last_row = (row < n_ctx // ROW - 1).astype(F32)
    early, late, before = -core, 1 - core, -1 - core
    m_in = same(early, late)
    m_before = same(early, before) * (me - core > 0).astype(F32)
    kappa = []
    for c in range(4):
        value = same(2 * c + 1 - spot, 2 * c - 1 - spot)
        kappa.append(value * first_chip if c == 0 else value)

    prev_ids = idr[REACH - 1]
    prev_rows = jnp.transpose(jnp.broadcast_to(prev_ids.astype(F32), (SEG, SEG)))
    s_pos = lax.broadcasted_iota(jnp.int32, (SEG, SEG), 0)
    t_pos = lax.broadcasted_iota(jnp.int32, (SEG, SEG), 1)
    cut = jnp.full((SEG, SEG), -1e30, F32)
    open_ = jnp.zeros((SEG, SEG), F32)
    shut = (1.0 - not_first) * -1e30
    bias[0] = jnp.where((s_pos > t_pos) & (prev_rows == own_cols), open_, cut) + shut
    bias[1] = jnp.where((s_pos <= t_pos) & (own_rows == own_cols), open_, cut)
    um[...] = (own_rows == prev_ids[:, SEG - 1 :].astype(F32)).astype(F32) * not_first

    def combine(x, xp, tc, ta, ss, rs, c_own, c_other):
        base = core * 8
        for i in range(8):
            tc[i] = (x[base + i].astype(F32) * c_own + xp[i].astype(F32) * c_other).astype(BF16)
        for i in range(2):
            ta[2 * y + i] = tc[2 * y + i]
        for dy in range(1, 4):
            a2a(tc, ta, ss, rs, 1, dy, True).start()

    def a2a(src, dst, ss, rs, slot, dy, sending):
        to_y = lax.rem(y + dy, 4)
        from_y = y if sending else lax.rem(y - dy + 4, 4)
        index = slot + dy - 1
        return remote(
            src.at[pl.ds(2 * to_y, 2)], dst.at[pl.ds(2 * from_y, 2)],
            ss.at[index], rs.at[index], {"ctx": row * ROW + 2 * to_y + core},
        )

    def ring_out(ta, ro, ri, tc, ss, rs, forward):
        for dy in range(1, 4):
            a2a(tc, ta, ss, rs, 1, dy, False).wait_recv()
        for i in range(2):
            total = None
            for c in range(4) if forward else range(3, -1, -1):
                block = ta[2 * c + i].astype(F32)
                total = block if total is None else block + kappa[c] * total
            ro[i] = total.astype(BF16)
        remote(ro, ri, ss.at[4], rs.at[4], at(ROW if forward else -ROW)).start()

    def spread(ta, ro, ri, po, pc, ss, rs, forward):
        remote(ro, ri, ss.at[4], rs.at[4], at(ROW if forward else -ROW)).wait_recv()
        gate_in_row = first_chip if forward else last_row
        for i in range(2):
            state = ri[i].astype(F32) * gate_in_row
            for c in range(4) if forward else range(3, -1, -1):
                po[2 * c + i] = state.astype(BF16)
                state = ta[2 * c + i].astype(F32) + kappa[c] * state
        for i in range(2):
            pc[2 * y + i] = po[2 * y + i]
        for dy in range(1, 4):
            a2a(po, pc, ss, rs, 5, dy, True).start()

    def finish_start(x, xp, po, pc, sx, res, ss, rs, r_other, r_state, s_own, s_state):
        for dy in range(1, 4):
            a2a(po, pc, ss, rs, 5, dy, False).wait_recv()
        base = core * 8
        for i in range(8):
            state = pc[i].astype(F32)
            sx[i] = (x[base + i].astype(F32) * s_own + state * s_state).astype(BF16)
        final(sx, res, ss, rs).start()
        for i in range(8):
            state = pc[i].astype(F32)
            res[base + i] = (xp[i].astype(F32) * r_other + state * r_state).astype(BF16)

    def final(sx, res, ss, rs, sending=True):
        base = pl.multiple_of((core if sending else 1 - core) * 8, 8)
        return remote(sx, res.at[pl.ds(base, 8)], ss.at[8], rs.at[8], at(1 - 2 * core))

    f_pair.wait_recv()
    combine(fx, fxp, ftc, fta, f_ss, f_rs, is_late + is_early * m_in, is_early + is_late * m_in)

    for d in range(1, REACH + 1):
        remote(zt, zr.at[d - 1], z_ss.at[d - 1], z_rs.at[d - 1], at(d)).wait_recv()
    total = jnp.zeros((HEADS, 1, DIM), F32)
    for d in range(1, REACH + 1):
        weight = same(-d, -1) * (me >= d).astype(F32)
        total = total + zr[d - 1] * weight
    zb[...] = total
    loads[3].wait()
    loads[4].wait()

    def state_part(h, carry):
        lifted = (feature(q_s[:, columns(h)].astype(F32)) * um[...]).astype(BF16)
        fq[h] = lifted
        totals = jnp.broadcast_to(zb[h], (DIM, DIM)).astype(BF16)
        den = dot_nt(lifted, totals)
        den_s[h] = den
        scaled = g_s[:, columns(h)].astype(F32) * gt[h] / jnp.maximum(den, 1.0)
        bx[place_of(h)] = dot_tn(lifted, scaled.astype(BF16)).astype(BF16)
        return carry

    lax.fori_loop(0, HEADS, state_part, 0, unroll=2)
    b_pair = pair_send(bx, bxp, b_ss, b_rs)
    b_pair.start()

    scaling = DIM ** -0.5
    scale2 = scaling * math.log2(math.e)

    def local(h, carry):
        remote(k_s.at[:, columns(h)], kp.at[h], k_ss.at[h], k_rs.at[h], at(1)).wait_recv()
        remote(v_s.at[:, columns(h)], vp.at[h], v_ss.at[h], v_rs.at[h], at(1)).wait_recv()
        q = q_s[:, columns(h)]
        k = k_s[:, columns(h)]
        v = v_s[:, columns(h)]
        keys, values = kp[h], vp[h]
        ga = (g_s[:, columns(h)].astype(F32) * (1.0 - gt[h])).astype(BF16)
        s0 = dot_nt(keys, q) * scale2 + bias[0]
        s1 = dot_nt(k, q) * scale2 + bias[1]
        top = jnp.max(jnp.maximum(s0, s1), axis=0, keepdims=True)
        e0 = jnp.exp2(s0 - top)
        e1 = jnp.exp2(s1 - top)
        inverse = 1.0 / jnp.sum(e0 + e1, axis=0, keepdims=True)
        w0 = e0 * inverse
        w1 = e1 * inverse
        gw0 = dot_nt(values, ga)
        gw1 = dot_nt(v, ga)
        delta = jnp.sum(w0 * gw0 + w1 * gw1, axis=0, keepdims=True)
        ds0 = (w0 * (gw0 - delta) * scaling).astype(BF16)
        ds1 = (w1 * (gw1 - delta) * scaling).astype(BF16)
        wb0 = w0.astype(BF16)
        wb1 = w1.astype(BF16)
        dks[h] = dot_nn(ds0, q).astype(BF16)
        dvs[h] = dot_nn(wb0, ga).astype(BF16)
        ol[h] = dot_tn(wb0, values) + dot_tn(wb1, v)
        dql[h] = dot_tn(ds0, keys) + dot_tn(ds1, k)
        dkl[h] = dot_nn(ds1, q)
        dvl[h] = dot_nn(wb1, ga)
        remote(dks.at[h], dkn.at[h], dk_ss.at[h], dk_rs.at[h], at(-1)).start()
        remote(dvs.at[h], dvn.at[h], dv_ss.at[h], dv_rs.at[h], at(-1)).start()
        return carry

    def local_heads(low, high):
        lax.fori_loop(low, high, local, 0)

    local_heads(0, 3)
    ring_out(fta, fro, fri, ftc, f_ss, f_rs, True)
    b_pair.wait_recv()
    combine(bx, bxp, btc, bta, b_ss, b_rs, is_early + is_late * m_before, is_late + is_early * m_before)
    local_heads(3, 6)
    spread(fta, fro, fri, fpo, fpc, f_ss, f_rs, True)
    ring_out(bta, bro, bri, btc, b_ss, b_rs, False)
    local_heads(6, 10)
    finish_start(
        fx, fxp, fpo, fpc, fsx, fres, f_ss, f_rs,
        is_late, is_early + is_late * m_before, is_early, is_late + is_early * m_before,
    )
    spread(bta, bro, bri, bpo, bpc, b_ss, b_rs, False)
    local_heads(10, HEADS)
    final(fsx, fres, f_ss, f_rs, False).wait_recv()

    def reads(h, carry):
        state = fres[place_of(h)]
        lifted = fq[h]
        den = den_s[h]
        inverse = 1.0 / jnp.maximum(den, 1.0)
        gate = gt[h]
        grad = g_s[:, columns(h)].astype(F32)
        out = dot_nn(lifted, state) * inverse
        near_out = ol[h]
        att_o[:, columns(h)] = (gate * out + (1.0 - gate) * near_out).astype(BF16)
        rows = jnp.sum(grad * (out - near_out), axis=0, keepdims=True)
        gg[h] = rows * (gate * (1.0 - gate))
        scaled_grad = grad * gate
        active = jnp.where(den > 1.0, 1.0, jnp.where(den == 1.0, 0.5, 0.0))
        dden = -jnp.sum(scaled_grad * out, axis=1, keepdims=True) * inverse * active
        back = dot_nt((scaled_grad * inverse).astype(BF16), state) + dden * zb[h]
        wide = lifted.astype(F32)
        dzt[h] = jnp.sum(dden * wide, axis=0, keepdims=True)
        dq_o[:, columns(h)] = (dql[h] + back * jnp.minimum(wide, 1.0)).astype(BF16)
        return carry

    lax.fori_loop(0, HEADS, reads, 0, unroll=2)
    for d in range(1, REACH + 1):
        remote(dzt, dzr.at[d - 1], dz_ss.at[d - 1], dz_rs.at[d - 1], at(-d)).start()

    lane = lax.broadcasted_iota(jnp.int32, (1, DIM), 1)
    mine = jnp.zeros((1, DIM), F32)
    for h in range(HEADS):
        mine = mine + jnp.where(lane == h, jnp.sum(gg[h], axis=1, keepdims=True), 0.0)
    red_s[0] = mine

    def row_copy(d):
        to = {"ctx": row * ROW + lax.rem(spot + d, ROW)}
        return remote(red_s.at[0], red_r.at[d - 1], red_ss.at[d - 1], red_rs.at[d - 1], to)

    for d in range(1, ROW):
        row_copy(d).start()
    copies_out = [
        pltpu.make_async_copy(att_o, att_out, out_sem.at[0]),
        pltpu.make_async_copy(dq_o, dq_out, out_sem.at[1]),
    ]
    for copy in copies_out:
        copy.start()

    finish_start(
        bx, bxp, bpo, bpc, bsx, bres, b_ss, b_rs,
        is_early, is_late + is_early * m_in, is_late, is_early + is_late * m_in,
    )
    for d in range(1, ROW):
        row_copy(d).wait_recv()
        mine = mine + red_r[d - 1]
    red_s[1] = mine

    n_rows = n_ctx // ROW

    def x_copy(d):
        i = ROW - 1 + d - 1
        return remote(red_s.at[1], red_r.at[i], red_ss.at[i], red_rs.at[i], at(ROW * d))

    for d in range(1, n_rows):
        x_copy(d).start()

    for d in range(1, REACH + 1):
        remote(dzt, dzr.at[d - 1], dz_ss.at[d - 1], dz_rs.at[d - 1], at(-d)).wait_recv()
    total = jnp.zeros((HEADS, 1, DIM), F32)
    for d in range(1, REACH + 1):
        weight = same(d - 1, 0) * (me + d < n_ctx).astype(F32)
        total = total + dzr[d - 1] * weight
    cz[...] = total

    for d in range(1, n_rows):
        x_copy(d).wait_recv()
        mine = mine + red_r[ROW - 1 + d - 1]

    def z_copy(i, d):
        j = ROW - 1 + n_rows - 1 + i
        return remote(red_s.at[2 + i], red_r.at[j], red_ss.at[j], red_rs.at[j], up(d))

    def z_begin(i):
        red_s[2 + i] = mine
        z_copy(i, steps_z[i]).start()

    def z_end(i):
        z_copy(i, steps_z[i]).wait_recv()
        return mine + red_r[ROW - 1 + n_rows - 1 + i]

    if steps_z:
        z_begin(0)
    final(bsx, bres, b_ss, b_rs, False).wait_recv()

    def writes(h, carry):
        remote(dks.at[h], dkn.at[h], dk_ss.at[h], dk_rs.at[h], at(-1)).wait_recv()
        remote(dvs.at[h], dvn.at[h], dv_ss.at[h], dv_rs.at[h], at(-1)).wait_recv()
        carried = bres[place_of(h)]
        lifted = fk[h]
        back = dot_nt(v_s[:, columns(h)], carried) + cz[h]
        mem_key = back * jnp.minimum(lifted.astype(F32), 1.0)
        dk_o[:, columns(h)] = (dkl[h] + dkn[h].astype(F32) + mem_key).astype(BF16)
        mem_value = dot_nn(lifted, carried)
        dv_o[:, columns(h)] = (dvl[h] + dvn[h].astype(F32) + mem_value).astype(BF16)
        return carry

    pieces = max(1, len(steps_z))
    for i in range(pieces):
        lax.fori_loop(i * HEADS // pieces, (i + 1) * HEADS // pieces, writes, 0)
        if steps_z:
            mine = z_end(i)
            if i + 1 < len(steps_z):
                z_begin(i + 1)
    gg_out[...] = mine[:, :HEADS]
    copies_out += [
        pltpu.make_async_copy(dk_o, dk_out, out_sem.at[2]),
        pltpu.make_async_copy(dv_o, dv_out, out_sem.at[3]),
    ]
    for copy in copies_out[2:]:
        copy.start()

    for i, d in enumerate(steps_z):
        z_copy(i, d).wait_send()
    for d in range(1, n_rows):
        x_copy(d).wait_send()
    for d in range(1, ROW):
        row_copy(d).wait_send()
    for d in range(1, REACH + 1):
        remote(zt, zr.at[d - 1], z_ss.at[d - 1], z_rs.at[d - 1], at(d)).wait_send()
        remote(dzt, dzr.at[d - 1], dz_ss.at[d - 1], dz_rs.at[d - 1], at(-d)).wait_send()
    for x, xp, tc, ta, ro, ri, po, pc, sx, res, ss, rs, forward in (
        (fx, fxp, ftc, fta, fro, fri, fpo, fpc, fsx, fres, f_ss, f_rs, True),
        (bx, bxp, btc, bta, bro, bri, bpo, bpc, bsx, bres, b_ss, b_rs, False),
    ):
        pair_send(x, xp, ss, rs).wait_send()
        for dy in range(1, 4):
            a2a(tc, ta, ss, rs, 1, dy, True).wait_send()
            a2a(po, pc, ss, rs, 5, dy, True).wait_send()
        remote(ro, ri, ss.at[4], rs.at[4], at(ROW if forward else -ROW)).wait_send()
        final(sx, res, ss, rs).wait_send()

    def drain(h, carry):
        remote(k_s.at[:, columns(h)], kp.at[h], k_ss.at[h], k_rs.at[h], at(1)).wait_send()
        remote(v_s.at[:, columns(h)], vp.at[h], v_ss.at[h], v_rs.at[h], at(1)).wait_send()
        remote(dks.at[h], dkn.at[h], dk_ss.at[h], dk_rs.at[h], at(-1)).wait_send()
        remote(dvs.at[h], dvn.at[h], dv_ss.at[h], dv_rs.at[h], at(-1)).wait_send()
        return carry

    lax.fori_loop(0, HEADS, drain, 0)
    for copy in copies_out:
        copy.wait()


def on_device(n_ctx, n_dp, queries, key_rows, value_rows, doc_ids, gate_logit, grad_out):
    flat = (SEG, HEADS * DIM)
    blocks = (HEADS, DIM, DIM)
    wide = jax.ShapeDtypeStruct(flat, BF16)
    anywhere = pl.BlockSpec(memory_space=pl.ANY)
    half = pltpu.VMEM(blocks, BF16)
    full = pltpu.VMEM(blocks, F32)

    def part(n):
        return pltpu.VMEM((n, DIM, DIM), BF16)

    lanes = pltpu.VMEM((HEADS, 1, DIM), F32)
    reach = pltpu.VMEM((REACH, HEADS, 1, DIM), F32)
    rows = pltpu.VMEM(flat, BF16)
    steps = max(1, n_dp.bit_length() - 1)
    n_red = ROW - 1 + n_ctx // ROW - 1 + steps
    exchange = [half, part(8), part(8), part(8), part(2), part(2), part(8), part(8), part(8), half]
    dma = pltpu.SemaphoreType.DMA
    scratch = (
        [rows] * 4
        + [pltpu.VMEM((2 * REACH + 1, 1, DIM), jnp.int32)]
        + [half] * 4 + [full]
        + exchange + exchange
        + [full] * 4 + [half] * 4
        + [rows] * 4
        + [lanes, reach, lanes, lanes, reach, lanes, lanes, lanes]
        + [pltpu.VMEM((2, SEG, SEG), F32), pltpu.VMEM((SEG, SEG), F32), pltpu.VMEM((SEG, DIM), F32)]
        + [pltpu.VMEM((2 + steps, 1, DIM), F32), pltpu.VMEM((n_red, 1, DIM), F32)]
        + [dma((5,)), dma((4,)), dma((15,)), dma((15,))]
        + [dma((REACH,))] * 4
        + [dma((HEADS,))] * 8
        + [dma((9,))] * 4
        + [dma((n_red,))] * 2
    )
    results = pl.pallas_call(
        functools.partial(kernel, n_ctx, n_dp),
        out_shape=[wide, wide, wide, wide, jax.ShapeDtypeStruct((1, HEADS), F32)],
        in_specs=[
            anywhere, anywhere, anywhere, anywhere,
            pl.BlockSpec(memory_space=pltpu.SMEM), anywhere,
        ],
        out_specs=[anywhere] * 4 + [pl.BlockSpec(memory_space=pltpu.VMEM)],
        scratch_shapes=scratch,
        compiler_params=pltpu.CompilerParams(
            collective_id=0, has_side_effects=True, vmem_limit_bytes=60 * 2**20
        ),
    )(
        queries.reshape(flat), key_rows.reshape(flat), value_rows.reshape(flat),
        doc_ids.reshape(1, SEG), gate_logit.reshape(1, HEADS), grad_out.reshape(flat),
    )
    shape = (1,) + flat
    return tuple(r.reshape(shape) for r in results[:4]) + (results[4].reshape(HEADS),)


def solution(mesh):
    tokens = P("dp", "ctx", None)
    return jax.shard_map(
        functools.partial(on_device, mesh.shape["ctx"], mesh.shape["dp"]),
        mesh=mesh,
        in_specs=(tokens, tokens, tokens, P("dp", "ctx"), P(), tokens),
        out_specs=(tokens, tokens, tokens, tokens, P()),
        check_vma=False,
    )
```

```python
import functools
import math

import jax
import jax.numpy as jnp
from jax import lax
from jax.experimental import pallas as pl
from jax.experimental.pallas import tpu as pltpu
from jax.sharding import PartitionSpec as P

SEG = 128
DIM = 128
HEADS = 16
ROW = 8
REACH = 8
UNROLL = 2
SCOPED = 103 * 2**19
MESH = pl.DeviceIdType.MESH
F32 = jnp.float32
BF16 = jnp.bfloat16


def dot_nn(a, b):
    return lax.dot_general(a, b, (((1,), (0,)), ((), ())), preferred_element_type=F32)


def dot_nt(a, b):
    return lax.dot_general(a, b, (((1,), (1,)), ((), ())), preferred_element_type=F32)


def dot_tn(a, b):
    return lax.dot_general(a, b, (((0,), (0,)), ((), ())), preferred_element_type=F32)


def place_of(h):
    return lax.rem(lax.div(h, 2), 2) * 8 + lax.div(h, 4) * 2 + lax.rem(h, 2)


def columns(h):
    return pl.ds(pl.multiple_of(h * DIM, DIM), DIM)


def feature(x):
    return jnp.where(x > 0, x + 1.0, jnp.exp(jnp.minimum(x, 0.0)))


def kernel(
    n_ctx, n_dp,
    q_in, k_in, v_in, ids_in, gate_in, g_in,
    att_out, dq_out, dk_out, dv_out, gg_out,
    q_s, k_s, v_s, g_s, idr, kp, vp, fk, fq, inv_s, den_s,
    fx, fxp, ftc, fta, fro, fri, fpo, fpc, fsx, fres,
    bx, bxp, btc, bta, bro, bri, bpo, bpc, bsx, bres,
    ol, dql, dkl, dvl, dks, dvs, dkn, dvn, att_o, dq_o, dk_o, dv_o,
    zt, zr, zb, dzt, dzr, cz, gt, gg, bias, wm, um,
    red_s, red_r,
    load_sem, out_sem, ready, ids_ss, ids_rs, z_ss, z_rs, dz_ss, dz_rs,
    k_ss, k_rs, v_ss, v_rs, dk_ss, dk_rs, dv_ss, dv_rs,
    f_ss, f_rs, b_ss, b_rs, red_ss, red_rs,
):
    me = lax.axis_index("ctx")
    mz = lax.axis_index("dp")
    row = lax.div(me, ROW)
    spot = lax.rem(me, ROW)
    y = lax.div(spot, 2)
    core = lax.rem(me, 2)

    def at(offset):
        return {"ctx": lax.rem(me + offset + n_ctx, n_ctx)}

    def up(offset):
        return {"dp": lax.rem(mz + offset + n_dp, n_dp)}

    def remote(src, dst, ss, rs, device):
        return pltpu.make_async_remote_copy(
            src_ref=src, dst_ref=dst, send_sem=ss, recv_sem=rs,
            device_id=device, device_id_type=MESH,
        )

    quarter = HEADS * DIM // 4
    loads = []
    for i in range(4):
        part = pl.ds(i * quarter, quarter)
        loads.append(pltpu.make_async_copy(k_in.at[:, part], k_s.at[:, part], load_sem.at[i]))
    for i, (src, dst) in enumerate(((ids_in, idr.at[REACH]), (v_in, v_s), (q_in, q_s), (g_in, g_s))):
        loads.append(pltpu.make_async_copy(src, dst, load_sem.at[4 + i]))
    for copy in loads[4:5] + loads[:4]:
        copy.start()
    barrier = pltpu.get_barrier_semaphore()
    near = [d for d in range(-REACH, REACH + 1) if d] + [n_ctx // 2]
    far = [1, n_dp - 1] if n_dp > 2 else []
    hops = list(range(1, n_dp)) if far else []
    for d in near:
        pl.semaphore_signal(barrier, inc=1, device_id=at(d), device_id_type=MESH)
    for d in far:
        pl.semaphore_signal(barrier, inc=1, device_id=up(d), device_id_type=MESH)

    loads[5].start()
    for h in range(HEADS):
        logit = jnp.full((1, DIM), gate_in[0, h], F32)
        gt[h] = 1.0 / (1.0 + jnp.exp(-logit))
    loads[4].wait()
    own_ids = idr[REACH]
    own_cols = jnp.broadcast_to(own_ids.astype(F32), (SEG, SEG))
    own_rows = jnp.transpose(own_cols)
    own_last = own_ids[:, SEG - 1 :].astype(F32)
    wm[...] = (own_rows == own_last).astype(F32)
    def lift(h, carry):
        lifted = feature(k_s[:, columns(h)].astype(F32)) * wm[...]
        fk[h] = lifted.astype(BF16)
        zt[h] = jnp.sum(lifted, axis=0, keepdims=True)
        return carry

    for i in range(4):
        loads[i].wait()
        lax.fori_loop(4 * i, 4 * i + 4, lift, 0, unroll=4)
    for copy in loads[6:]:
        copy.start()
    pl.semaphore_wait(barrier, len(near) + len(far))

    id_sends = [d for d in range(-(REACH - 1), REACH + 1) if d]
    for i, d in enumerate(id_sends):
        remote(idr.at[REACH], idr.at[REACH - d], ids_ss.at[i], ids_rs.at[i], at(d)).start()
    for d in range(1, REACH + 1):
        remote(zt, zr.at[d - 1], z_ss.at[d - 1], z_rs.at[d - 1], at(d)).start()
    def tell(i):
        if far:
            for d in (2**i, -(2**i)):
                pl.semaphore_signal(ready.at[i], inc=1, device_id=up(d), device_id_type=MESH)

    def told(i):
        if far:
            pl.semaphore_wait(ready.at[i], 2)

    tell(0)

    def send_kv(h, carry):
        remote(k_s.at[:, columns(h)], kp.at[h], k_ss.at[h], k_rs.at[h], at(1)).start()
        remote(v_s.at[:, columns(h)], vp.at[h], v_ss.at[h], v_rs.at[h], at(1)).start()
        return carry

    loads[5].wait()
    for h in range(4):
        send_kv(h, 0)

    def tails(h, carry):
        fx[place_of(h)] = dot_tn(fk[h], v_s[:, columns(h)]).astype(BF16)
        return carry

    lax.fori_loop(0, HEADS, tails, 0, unroll=4)

    def pair_send(x, xp, ss, rs):
        other = pl.ds(pl.multiple_of((1 - core) * 8, 8), 8)
        return remote(x.at[other], xp, ss.at[0], rs.at[0], at(1 - 2 * core))

    f_pair = pair_send(fx, fxp, f_ss, f_rs)
    f_pair.start()

    def await_ids(near_by):
        for i, d in enumerate(id_sends):
            if (abs(d) == 1) == near_by:
                remote(idr.at[REACH], idr.at[REACH - d], ids_ss.at[i], ids_rs.at[i], at(d)).wait()

    await_ids(True)

    def last(offset):
        return idr[REACH + offset][:, SEG - 1 :]

    def same(a, b):
        return (last(a) == last(b)).astype(F32)

    is_late = core.astype(F32)
    is_early = 1.0 - is_late
    not_first = (me > 0).astype(F32)
    first_chip = (row > 0).astype(F32)
    last_row = (row < n_ctx // ROW - 1).astype(F32)
    early, late, before = -core, 1 - core, -1 - core
    m_in = same(early, late)

    def far_masks():
        kappa = []
        for c in range(4):
            value = same(2 * c + 1 - spot, 2 * c - 1 - spot)
            kappa.append(value * first_chip if c == 0 else value)
        return kappa, same(early, before) * (me - core > 0).astype(F32)

    prev_ids = idr[REACH - 1]
    prev_rows = jnp.transpose(jnp.broadcast_to(prev_ids.astype(F32), (SEG, SEG)))
    s_pos = lax.broadcasted_iota(jnp.int32, (SEG, SEG), 0)
    t_pos = lax.broadcasted_iota(jnp.int32, (SEG, SEG), 1)
    cut = jnp.full((SEG, SEG), -1e30, F32)
    open_ = jnp.zeros((SEG, SEG), F32)
    shut = (1.0 - not_first) * -1e30
    bias[0] = jnp.where((s_pos > t_pos) & (prev_rows == own_cols), open_, cut) + shut
    bias[1] = jnp.where((s_pos <= t_pos) & (own_rows == own_cols), open_, cut)
    um[...] = (own_rows == prev_ids[:, SEG - 1 :].astype(F32)).astype(F32) * not_first

    def combine(x, xp, tc, ta, ss, rs, c_own, c_other):
        base = core * 8
        for i in range(8):
            tc[i] = (x[base + i].astype(F32) * c_own + xp[i].astype(F32) * c_other).astype(BF16)
        for i in range(2):
            ta[2 * y + i] = tc[2 * y + i]
        for dy in range(1, 4):
            a2a(tc, ta, ss, rs, 1, dy, True).start()

    def a2a(src, dst, ss, rs, slot, dy, sending):
        to_y = lax.rem(y + dy, 4)
        from_y = y if sending else lax.rem(y - dy + 4, 4)
        index = slot + dy - 1
        return remote(
            src.at[pl.ds(2 * to_y, 2)], dst.at[pl.ds(2 * from_y, 2)],
            ss.at[index], rs.at[index], {"ctx": row * ROW + 2 * to_y + core},
        )

    def ring_out(ta, ro, ri, tc, ss, rs, forward):
        for dy in range(1, 4):
            a2a(tc, ta, ss, rs, 1, dy, False).wait_recv()
        for i in range(2):
            total = None
            for c in range(4) if forward else range(3, -1, -1):
                block = ta[2 * c + i].astype(F32)
                total = block if total is None else block + kappa[c] * total
            ro[i] = total.astype(BF16)
        remote(ro, ri, ss.at[4], rs.at[4], at(ROW if forward else -ROW)).start()

    def spread(ta, ro, ri, po, pc, ss, rs, forward):
        remote(ro, ri, ss.at[4], rs.at[4], at(ROW if forward else -ROW)).wait_recv()
        gate_in_row = first_chip if forward else last_row
        for i in range(2):
            state = ri[i].astype(F32) * gate_in_row
            for c in range(4) if forward else range(3, -1, -1):
                po[2 * c + i] = state.astype(BF16)
                state = ta[2 * c + i].astype(F32) + kappa[c] * state
        for i in range(2):
            pc[2 * y + i] = po[2 * y + i]
        for dy in range(1, 4):
            a2a(po, pc, ss, rs, 5, dy, True).start()

    def finish_start(x, xp, po, pc, sx, res, ss, rs, r_other, r_state, s_own, s_state):
        for dy in range(1, 4):
            a2a(po, pc, ss, rs, 5, dy, False).wait_recv()
        base = core * 8
        for i in range(8):
            state = pc[i].astype(F32)
            sx[i] = (x[base + i].astype(F32) * s_own + state * s_state).astype(BF16)
        final(sx, res, ss, rs).start()
        for i in range(8):
            state = pc[i].astype(F32)
            res[base + i] = (xp[i].astype(F32) * r_other + state * r_state).astype(BF16)

    def final(sx, res, ss, rs, sending=True):
        base = pl.multiple_of((core if sending else 1 - core) * 8, 8)
        return remote(sx, res.at[pl.ds(base, 8)], ss.at[8], rs.at[8], at(1 - 2 * core))

    f_pair.wait_recv()
    combine(fx, fxp, ftc, fta, f_ss, f_rs, is_late + is_early * m_in, is_early + is_late * m_in)
    loads[6].wait()
    loads[7].wait()
    scaling = DIM ** -0.5
    scale2 = scaling * math.log2(math.e)

    def local(h, carry):
        q = q_s[:, columns(h)]
        k = k_s[:, columns(h)]
        v = v_s[:, columns(h)]
        keys, values = kp[h], vp[h]
        ga = (g_s[:, columns(h)].astype(F32) * (1.0 - gt[h])).astype(BF16)
        s0 = dot_nt(keys, q) * scale2 + bias[0]
        s1 = dot_nt(k, q) * scale2 + bias[1]
        top = jnp.max(jnp.maximum(s0, s1), axis=0, keepdims=True)
        e0 = jnp.exp2(s0 - top)
        e1 = jnp.exp2(s1 - top)
        inverse = 1.0 / jnp.sum(e0 + e1, axis=0, keepdims=True)
        w0 = e0 * inverse
        w1 = e1 * inverse
        gw0 = dot_nt(values, ga)
        gw1 = dot_nt(v, ga)
        delta = jnp.sum(w0 * gw0 + w1 * gw1, axis=0, keepdims=True)
        ds0 = (w0 * (gw0 - delta) * scaling).astype(BF16)
        ds1 = (w1 * (gw1 - delta) * scaling).astype(BF16)
        wb0 = w0.astype(BF16)
        wb1 = w1.astype(BF16)
        dks[h] = dot_nn(ds0, q).astype(BF16)
        dvs[h] = dot_nn(wb0, ga).astype(BF16)
        out = dot_tn(wb0, values) + dot_tn(wb1, v)
        ol[h] = out
        gate = gt[h]
        rows = jnp.sum(g_s[:, columns(h)].astype(F32) * out, axis=0, keepdims=True)
        gg[h] = rows * (gate * (gate - 1.0))
        dql[h] = dot_tn(ds0, keys) + dot_tn(ds1, k)
        dkl[h] = dot_nn(ds1, q)
        dvl[h] = dot_nn(wb1, ga)
        return carry

    def send_back(h, carry):
        remote(dks.at[h], dkn.at[h], dk_ss.at[h], dk_rs.at[h], at(-1)).start()
        remote(dvs.at[h], dvn.at[h], dv_ss.at[h], dv_rs.at[h], at(-1)).start()
        return carry

    def arrived(h, carry):
        remote(k_s.at[:, columns(h)], kp.at[h], k_ss.at[h], k_rs.at[h], at(1)).wait_recv()
        remote(v_s.at[:, columns(h)], vp.at[h], v_ss.at[h], v_rs.at[h], at(1)).wait_recv()
        return carry

    def local_heads(low, more=()):
        for h in range(low, low + 2):
            arrived(h, 0)
        lax.fori_loop(low, low + 2, local, 0, unroll=UNROLL)
        for h in range(low, low + 2):
            send_back(h, 0)
        for h in more:
            send_kv(h, 0)

    await_ids(False)
    kappa, m_before = far_masks()
    told(0)
    tell(1)

    for d in range(1, REACH + 1):
        remote(zt, zr.at[d - 1], z_ss.at[d - 1], z_rs.at[d - 1], at(d)).wait_recv()
    total = jnp.zeros((HEADS, 1, DIM), F32)
    for d in range(1, REACH + 1):
        weight = same(-d, -1) * (me >= d).astype(F32)
        total = total + zr[d - 1] * weight
    zb[...] = total

    def state_part(h, carry):
        lifted = (feature(q_s[:, columns(h)].astype(F32)) * um[...]).astype(BF16)
        fq[h] = lifted
        totals = jnp.broadcast_to(zb[h], (DIM, DIM)).astype(BF16)
        den = dot_nt(lifted, totals)
        inverse = 1.0 / jnp.maximum(den, 1.0)
        inv_s[h] = inverse
        den_s[h] = den
        scaled = g_s[:, columns(h)].astype(F32) * gt[h] * inverse
        bx[place_of(h)] = dot_tn(lifted, scaled.astype(BF16)).astype(BF16)
        return carry

    for i in range(4):
        lax.fori_loop(4 * i, 4 * i + 4, state_part, 0, unroll=4)
        send_kv(4 + i, 0)
    b_pair = pair_send(bx, bxp, b_ss, b_rs)
    b_pair.start()

    def add_rows(h, rows):
        gg[h] = gg[h] + rows * (1.0 - gt[h])

    ring_out(fta, fro, fri, ftc, f_ss, f_rs, True)
    local_heads(0, (8,))
    b_pair.wait_recv()
    combine(bx, bxp, btc, bta, b_ss, b_rs, is_early + is_late * m_before, is_late + is_early * m_before)
    send_kv(9, 0)
    local_heads(2, (10,))
    told(1)
    tell(2)
    local_heads(4, (11,))
    spread(fta, fro, fri, fpo, fpc, f_ss, f_rs, True)
    local_heads(6, (12, 13))
    local_heads(8, (14, 15))
    ring_out(bta, bro, bri, btc, b_ss, b_rs, False)
    local_heads(10)
    local_heads(12)
    spread(bta, bro, bri, bpo, bpc, b_ss, b_rs, False)
    local_heads(14)

    for i in range(2):
        rows = jnp.zeros((1, DIM), F32)
        for c in range(4):
            product = bta[2 * c + i].astype(F32) * fpo[2 * c + i].astype(F32)
            rows = rows + jnp.sum(product, axis=0, keepdims=True)
        add_rows(2 * spot + i, rows)
    late_core = core == 1
    for i in range(8):
        grads = jnp.where(late_core, bx[core * 8 + i], bxp[i]).astype(F32)
        states = jnp.where(late_core, fxp[i], fx[core * 8 + i]).astype(F32)
        rows = jnp.sum(grads * states, axis=0, keepdims=True)
        add_rows(4 * (i // 2) + 2 * core + i % 2, rows)

    lane = lax.broadcasted_iota(jnp.int32, (1, DIM), 1)
    mine = jnp.zeros((1, DIM), F32)
    for h in range(HEADS):
        mine = mine + jnp.where(lane == h, jnp.sum(gg[h], axis=1, keepdims=True), 0.0)
    red_s[0] = mine

    n_rows = n_ctx // ROW

    def x_copy(d):
        i = d - 1
        return remote(red_s.at[0], red_r.at[i], red_ss.at[i], red_rs.at[i], at(ROW * d))

    def z_copy(d):
        j = n_rows - 1 + d - 1
        return remote(red_s.at[1], red_r.at[j], red_ss.at[j], red_rs.at[j], up(d))

    def row_copy(d):
        to = {"ctx": row * ROW + lax.rem(spot + d, ROW)}
        j = n_rows - 1 + n_dp - 1 + d - 1
        return remote(red_s.at[2], red_r.at[j], red_ss.at[j], red_rs.at[j], to)

    for d in range(1, n_rows):
        x_copy(d).start()
    finish_start(
        fx, fxp, fpo, fpc, fsx, fres, f_ss, f_rs,
        is_late, is_early + is_late * m_before, is_early, is_late + is_early * m_before,
    )
    told(2)
    for d in range(1, n_rows):
        x_copy(d).wait_recv()
        mine = mine + red_r[d - 1]
    red_s[1] = mine
    for d in hops:
        z_copy(d).start()
    final(fsx, fres, f_ss, f_rs, False).wait_recv()

    def reads(h, carry):
        state = fres[place_of(h)]
        lifted = fq[h]
        inverse = inv_s[h]
        gate = gt[h]
        grad = g_s[:, columns(h)].astype(F32)
        out = dot_nn(lifted, state) * inverse
        near_out = ol[h]
        att_o[:, columns(h)] = (gate * out + (1.0 - gate) * near_out).astype(BF16)
        scaled_grad = grad * gate
        den = den_s[h]
        active = jnp.where(den > 1.0, inverse, jnp.where(den == 1.0, 0.5, 0.0))
        dden = -jnp.sum(scaled_grad * out, axis=1, keepdims=True) * active
        back = dot_nt((scaled_grad * inverse).astype(BF16), state) + dden * zb[h]
        wide = lifted.astype(F32)
        dzt[h] = jnp.sum(dden * wide, axis=0, keepdims=True)
        dq_o[:, columns(h)] = (dql[h] + back * jnp.minimum(wide, 1.0)).astype(BF16)
        return carry

    lax.fori_loop(0, HEADS, reads, 0, unroll=4)
    for d in range(1, REACH + 1):
        remote(dzt, dzr.at[d - 1], dz_ss.at[d - 1], dz_rs.at[d - 1], at(-d)).start()

    half = HEADS * DIM // 2

    def put(i, which):
        src, dst = ((att_o, att_out), (dq_o, dq_out), (dk_o, dk_out), (dv_o, dv_out))[which]
        part = pl.ds(i * half, half)
        return pltpu.make_async_copy(src.at[:, part], dst.at[:, part], out_sem.at[2 * which + i])

    for i in range(2):
        put(i, 0).start()
        put(i, 1).start()
    finish_start(
        bx, bxp, bpo, bpc, bsx, bres, b_ss, b_rs,
        is_early, is_late + is_early * m_in, is_late, is_early + is_late * m_in,
    )

    for d in range(1, REACH + 1):
        remote(dzt, dzr.at[d - 1], dz_ss.at[d - 1], dz_rs.at[d - 1], at(-d)).wait_recv()
    total = jnp.zeros((HEADS, 1, DIM), F32)
    for d in range(1, REACH + 1):
        weight = same(d - 1, 0) * (me + d < n_ctx).astype(F32)
        total = total + dzr[d - 1] * weight
    cz[...] = total

    final(bsx, bres, b_ss, b_rs, False).wait_recv()

    def writes(h, carry):
        carried = bres[place_of(h)]
        lifted = fk[h]
        back = dot_nt(v_s[:, columns(h)], carried) + cz[h]
        mem_key = back * jnp.minimum(lifted.astype(F32), 1.0)
        dk_o[:, columns(h)] = (dkl[h] + dkn[h].astype(F32) + mem_key).astype(BF16)
        mem_value = dot_nn(lifted, carried)
        dv_o[:, columns(h)] = (dvl[h] + dvn[h].astype(F32) + mem_value).astype(BF16)
        return carry

    def returned(h, carry):
        remote(dks.at[h], dkn.at[h], dk_ss.at[h], dk_rs.at[h], at(-1)).wait_recv()
        remote(dvs.at[h], dvn.at[h], dv_ss.at[h], dv_rs.at[h], at(-1)).wait_recv()
        return carry

    for i in range(2):
        low, high = i * HEADS // 2, (i + 1) * HEADS // 2
        lax.fori_loop(low, high, returned, 0)
        lax.fori_loop(low, high, writes, 0, unroll=4)
        put(i, 2).start()
        put(i, 3).start()
    for d in hops:
        z_copy(d).wait_recv()
        mine = mine + red_r[n_rows - 1 + d - 1]
    red_s[2] = mine
    for d in range(1, ROW):
        row_copy(d).start()
    for d in range(1, ROW):
        row_copy(d).wait_recv()
        mine = mine + red_r[n_rows - 1 + n_dp - 1 + d - 1]
    gg_out[...] = mine[:, :HEADS]

    for d in hops:
        z_copy(d).wait_send()
    for d in range(1, n_rows):
        x_copy(d).wait_send()
    for d in range(1, ROW):
        row_copy(d).wait_send()
    for d in range(1, REACH + 1):
        remote(zt, zr.at[d - 1], z_ss.at[d - 1], z_rs.at[d - 1], at(d)).wait_send()
        remote(dzt, dzr.at[d - 1], dz_ss.at[d - 1], dz_rs.at[d - 1], at(-d)).wait_send()
    for x, xp, tc, ta, ro, ri, po, pc, sx, res, ss, rs, forward in (
        (fx, fxp, ftc, fta, fro, fri, fpo, fpc, fsx, fres, f_ss, f_rs, True),
        (bx, bxp, btc, bta, bro, bri, bpo, bpc, bsx, bres, b_ss, b_rs, False),
    ):
        pair_send(x, xp, ss, rs).wait_send()
        for dy in range(1, 4):
            a2a(tc, ta, ss, rs, 1, dy, True).wait_send()
            a2a(po, pc, ss, rs, 5, dy, True).wait_send()
        remote(ro, ri, ss.at[4], rs.at[4], at(ROW if forward else -ROW)).wait_send()
        final(sx, res, ss, rs).wait_send()

    def drain(h, carry):
        remote(k_s.at[:, columns(h)], kp.at[h], k_ss.at[h], k_rs.at[h], at(1)).wait_send()
        remote(v_s.at[:, columns(h)], vp.at[h], v_ss.at[h], v_rs.at[h], at(1)).wait_send()
        remote(dks.at[h], dkn.at[h], dk_ss.at[h], dk_rs.at[h], at(-1)).wait_send()
        remote(dvs.at[h], dvn.at[h], dv_ss.at[h], dv_rs.at[h], at(-1)).wait_send()
        return carry

    lax.fori_loop(0, HEADS, drain, 0)
    for i in range(2):
        for which in range(4):
            put(i, which).wait()


def write_out(*refs):
    ins, outs, sem = refs[:5], refs[5:10], refs[10]
    copies = [pltpu.make_async_copy(a, b, sem.at[i]) for i, (a, b) in enumerate(zip(ins, outs))]
    for copy in copies:
        copy.start()
    for copy in copies:
        copy.wait()


def on_device(n_ctx, n_dp, queries, key_rows, value_rows, doc_ids, gate_logit, grad_out):
    flat = (SEG, HEADS * DIM)
    blocks = (HEADS, DIM, DIM)
    wide = jax.ShapeDtypeStruct(flat, BF16)
    anywhere = pl.BlockSpec(memory_space=pltpu.HBM)
    vmem = pl.BlockSpec(memory_space=pltpu.VMEM)
    free = pl.BlockSpec(memory_space=pl.ANY)
    half = pltpu.VMEM(blocks, BF16)
    full = pltpu.VMEM(blocks, F32)

    def part(n):
        return pltpu.VMEM((n, DIM, DIM), BF16)

    lanes = pltpu.VMEM((HEADS, 1, DIM), F32)
    reach = pltpu.VMEM((REACH, HEADS, 1, DIM), F32)
    rows = pltpu.VMEM(flat, BF16)
    n_red = ROW - 1 + n_ctx // ROW - 1 + n_dp - 1
    exchange = [half, part(8), part(8), part(8), part(2), part(2), part(8), part(8), part(8), half]
    dma = pltpu.SemaphoreType.DMA
    scratch = (
        [rows] * 4
        + [pltpu.VMEM((2 * REACH + 1, 1, DIM), jnp.int32)]
        + [half] * 4 + [full] * 2
        + exchange + exchange
        + [full] * 4 + [half] * 4 + [rows] * 4
        + [lanes, reach, lanes, lanes, reach, lanes, lanes, lanes]
        + [pltpu.VMEM((2, SEG, SEG), F32), pltpu.VMEM((SEG, SEG), F32), pltpu.VMEM((SEG, DIM), F32)]
        + [pltpu.VMEM((3, 1, DIM), F32), pltpu.VMEM((n_red, 1, DIM), F32)]
        + [dma((8,)), dma((8,)), pltpu.SemaphoreType.REGULAR((3,)), dma((15,)), dma((15,))]
        + [dma((REACH,))] * 4
        + [dma((HEADS,))] * 8
        + [dma((9,))] * 4
        + [dma((n_red,))] * 2
    )
    shapes = [wide] * 4 + [jax.ShapeDtypeStruct((1, HEADS), F32)]
    results = pl.pallas_call(
        functools.partial(kernel, n_ctx, n_dp),
        out_shape=shapes,
        in_specs=[
            anywhere, anywhere, anywhere, anywhere,
            pl.BlockSpec(memory_space=pltpu.SMEM), anywhere,
        ],
        out_specs=[free] * 4 + [vmem],
        scratch_shapes=scratch,
        compiler_params=pltpu.CompilerParams(
            collective_id=0, has_side_effects=True, vmem_limit_bytes=SCOPED
        ),
    )(
        queries.reshape(flat), key_rows.reshape(flat), value_rows.reshape(flat),
        doc_ids.reshape(1, SEG), gate_logit.reshape(1, HEADS), grad_out.reshape(flat),
    )
    written = pl.pallas_call(
        write_out,
        out_shape=shapes,
        in_specs=[vmem] * 5,
        out_specs=[anywhere] * 5,
        scratch_shapes=[dma((5,))],
        compiler_params=pltpu.CompilerParams(vmem_limit_bytes=2**20),
    )(*results)
    shape = (1,) + flat
    return tuple(r.reshape(shape) for r in written[:4]) + (written[4].reshape(HEADS),)


def solution(mesh):
    tokens = P("dp", "ctx", None)
    return jax.shard_map(
        functools.partial(on_device, mesh.shape["ctx"], mesh.shape["dp"]),
        mesh=mesh,
        in_specs=(tokens, tokens, tokens, P("dp", "ctx"), P(), tokens),
        out_specs=(tokens, tokens, tokens, tokens, P()),
        check_vma=False,
    )
```

```python
import functools
import math

import jax
import jax.numpy as jnp
from jax import lax
from jax.experimental import pallas as pl
from jax.experimental.pallas import tpu as pltpu
from jax.sharding import PartitionSpec as P

SEG = 128
DIM = 128
HEADS = 16
ROW = 8
REACH = 8
UNROLL = 2
KV_AT = {"start": (0, 1), "f1": (2, 3, 4, 5), "s2": (6,), "b1": (7, 8, 9), "f2": (10, 11, 12), "l8": (13, 14, 15)}
BACK_AT = {f"l{h}": (h, h + 1) for h in range(0, 16, 2)}
SCOPED = 103 * 2**19
MESH = pl.DeviceIdType.MESH
F32 = jnp.float32
BF16 = jnp.bfloat16


def dot_nn(a, b):
    return lax.dot_general(a, b, (((1,), (0,)), ((), ())), preferred_element_type=F32)


def dot_nt(a, b):
    return lax.dot_general(a, b, (((1,), (1,)), ((), ())), preferred_element_type=F32)


def dot_tn(a, b):
    return lax.dot_general(a, b, (((0,), (0,)), ((), ())), preferred_element_type=F32)


def place_of(h):
    return lax.rem(lax.div(h, 2), 2) * 8 + lax.div(h, 4) * 2 + lax.rem(h, 2)


def columns(h):
    return pl.ds(pl.multiple_of(h * DIM, DIM), DIM)


def feature(x):
    return jnp.where(x > 0, x + 1.0, jnp.exp(jnp.minimum(x, 0.0)))


def kernel(
    n_ctx, n_dp,
    q_in, k_in, v_in, ids_in, gate_in, g_in,
    att_out, dq_out, dk_out, dv_out, gg_out,
    q_s, k_s, v_s, g_s, idr, kvp, fk, fq, inv_s, den_s,
    fx, fxp, ftc, fta, fro, fri, fpo, fpc, fsx, fres,
    bx, bxp, btc, bta, bro, bri, bpo, bpc, bsx, bres,
    ol, dql, dkl, dvl, dks, dvs, dkvn, att_o, dq_o, dk_o, dv_o,
    zt, zr, zb, dzt, dzr, cz, gt, gg, bias, wm, um,
    red_s, red_r,
    load_sem, out_sem, ready, sent, ids_rs, z_rs, dz_rs, kv_rs, dkv_rs,
    f_ss, f_rs, b_ss, b_rs, red_rs,
):
    me = lax.axis_index("ctx")
    mz = lax.axis_index("dp")
    row = lax.div(me, ROW)
    spot = lax.rem(me, ROW)
    y = lax.div(spot, 2)
    core = lax.rem(me, 2)

    def at(offset):
        return {"ctx": lax.rem(me + offset + n_ctx, n_ctx)}

    def up(offset):
        return {"dp": lax.rem(mz + offset + n_dp, n_dp)}

    def remote(src, dst, ss, rs, device):
        return pltpu.make_async_remote_copy(
            src_ref=src, dst_ref=dst, send_sem=ss, recv_sem=rs,
            device_id=device, device_id_type=MESH,
        )

    def arrival(ref, sem):
        pltpu.make_async_copy(ref, ref, sem).wait()

    quarter = HEADS * DIM // 4
    loads = []
    for i in range(4):
        part = pl.ds(i * quarter, quarter)
        loads.append(pltpu.make_async_copy(k_in.at[:, part], k_s.at[:, part], load_sem.at[i]))
    for i, (src, dst) in enumerate(((ids_in, idr.at[REACH]), (v_in, v_s), (q_in, q_s), (g_in, g_s))):
        loads.append(pltpu.make_async_copy(src, dst, load_sem.at[4 + i]))
    for copy in loads[4:5] + loads[:4]:
        copy.start()
    barrier = pltpu.get_barrier_semaphore()
    near = [d for d in range(-REACH, REACH + 1) if d] + [n_ctx // 2]
    far = [1, n_dp - 1] if n_dp > 2 else []
    hops = list(range(1, n_dp)) if far else []
    for d in near:
        pl.semaphore_signal(barrier, inc=1, device_id=at(d), device_id_type=MESH)
    for d in far:
        pl.semaphore_signal(barrier, inc=1, device_id=up(d), device_id_type=MESH)

    loads[5].start()
    for h in range(HEADS):
        logit = jnp.full((1, DIM), gate_in[0, h], F32)
        gt[h] = 1.0 / (1.0 + jnp.exp(-logit))
    loads[4].wait()
    own_ids = idr[REACH]
    own_cols = jnp.broadcast_to(own_ids.astype(F32), (SEG, SEG))
    own_rows = jnp.transpose(own_cols)
    own_last = own_ids[:, SEG - 1 :].astype(F32)
    wm[...] = (own_rows == own_last).astype(F32)
    def lift(h, carry):
        lifted = feature(k_s[:, columns(h)].astype(F32)) * wm[...]
        fk[h] = lifted.astype(BF16)
        zt[h] = jnp.sum(lifted, axis=0, keepdims=True)
        return carry

    for i in range(4):
        loads[i].wait()
        lax.fori_loop(4 * i, 4 * i + 4, lift, 0, unroll=4)
    for copy in loads[6:]:
        copy.start()
    pl.semaphore_wait(barrier, len(near) + len(far))

    id_sends = [d for d in range(-(REACH - 1), REACH + 1) if d]
    for i, d in enumerate(id_sends):
        which = {1: 0, -1: 1}.get(d, 2)
        remote(idr.at[REACH], idr.at[REACH - d], sent.at[2], ids_rs.at[which], at(d)).start()
    for d in range(1, REACH + 1):
        remote(zt, zr.at[d - 1], sent.at[3], z_rs, at(d)).start()
    def tell(i):
        if far:
            for d in (2**i, -(2**i)):
                pl.semaphore_signal(ready.at[i], inc=1, device_id=up(d), device_id_type=MESH)

    def told(i):
        if far:
            pl.semaphore_wait(ready.at[i], 2)

    tell(0)

    def send_kv(h, carry):
        remote(k_s.at[:, columns(h)], kvp.at[h, 0], sent.at[0], kv_rs.at[h], at(1)).start()
        remote(v_s.at[:, columns(h)], kvp.at[h, 1], sent.at[0], kv_rs.at[h], at(1)).start()
        return carry

    def send_back(h, carry):
        remote(dks.at[h], dkvn.at[h, 0], sent.at[1], dkv_rs.at[h], at(-1)).start()
        remote(dvs.at[h], dkvn.at[h, 1], sent.at[1], dkv_rs.at[h], at(-1)).start()
        return carry

    def bulk(where):
        for h in KV_AT.get(where, ()):
            send_kv(h, 0)
        for h in BACK_AT.get(where, ()):
            send_back(h, 0)

    loads[5].wait()
    bulk("start")

    def tails(h, carry):
        fx[place_of(h)] = dot_tn(fk[h], v_s[:, columns(h)]).astype(BF16)
        return carry

    lax.fori_loop(0, HEADS, tails, 0, unroll=4)

    def pair_send(x, xp, ss, rs):
        other = pl.ds(pl.multiple_of((1 - core) * 8, 8), 8)
        return remote(x.at[other], xp, ss.at[0], rs.at[0], at(1 - 2 * core))

    f_pair = pair_send(fx, fxp, f_ss, f_rs)
    f_pair.start()

    def await_ids(near_by):
        if near_by:
            arrival(idr.at[REACH - 1], ids_rs.at[0])
            arrival(idr.at[REACH + 1], ids_rs.at[1])
        else:
            arrival(idr.at[pl.ds(0, len(id_sends) - 2)], ids_rs.at[2])

    await_ids(True)

    def last(offset):
        return idr[REACH + offset][:, SEG - 1 :]

    def same(a, b):
        return (last(a) == last(b)).astype(F32)

    is_late = core.astype(F32)
    is_early = 1.0 - is_late
    not_first = (me > 0).astype(F32)
    first_chip = (row > 0).astype(F32)
    last_row = (row < n_ctx // ROW - 1).astype(F32)
    early, late, before = -core, 1 - core, -1 - core
    m_in = same(early, late)

    def far_masks():
        kappa = []
        for c in range(4):
            value = same(2 * c + 1 - spot, 2 * c - 1 - spot)
            kappa.append(value * first_chip if c == 0 else value)
        return kappa, same(early, before) * (me - core > 0).astype(F32)

    prev_ids = idr[REACH - 1]
    prev_rows = jnp.transpose(jnp.broadcast_to(prev_ids.astype(F32), (SEG, SEG)))
    s_pos = lax.broadcasted_iota(jnp.int32, (SEG, SEG), 0)
    t_pos = lax.broadcasted_iota(jnp.int32, (SEG, SEG), 1)
    cut = jnp.full((SEG, SEG), -1e30, F32)
    open_ = jnp.zeros((SEG, SEG), F32)
    shut = (1.0 - not_first) * -1e30
    bias[0] = jnp.where((s_pos > t_pos) & (prev_rows == own_cols), open_, cut) + shut
    bias[1] = jnp.where((s_pos <= t_pos) & (own_rows == own_cols), open_, cut)
    um[...] = (own_rows == prev_ids[:, SEG - 1 :].astype(F32)).astype(F32) * not_first

    def combine(x, xp, tc, ta, ss, rs, c_own, c_other):
        base = core * 8
        for i in range(8):
            tc[i] = (x[base + i].astype(F32) * c_own + xp[i].astype(F32) * c_other).astype(BF16)
        for i in range(2):
            ta[2 * y + i] = tc[2 * y + i]
        for dy in range(1, 4):
            a2a(tc, ta, ss, rs, 1, dy, True).start()

    def a2a(src, dst, ss, rs, slot, dy, sending):
        to_y = lax.rem(y + dy, 4)
        from_y = y if sending else lax.rem(y - dy + 4, 4)
        index = slot + dy - 1
        return remote(
            src.at[pl.ds(2 * to_y, 2)], dst.at[pl.ds(2 * from_y, 2)],
            ss.at[index], rs.at[index], {"ctx": row * ROW + 2 * to_y + core},
        )

    def ring_out(ta, ro, ri, tc, ss, rs, forward):
        for dy in range(1, 4):
            a2a(tc, ta, ss, rs, 1, dy, False).wait_recv()
        for i in range(2):
            total = None
            for c in range(4) if forward else range(3, -1, -1):
                block = ta[2 * c + i].astype(F32)
                total = block if total is None else block + kappa[c] * total
            ro[i] = total.astype(BF16)
        remote(ro, ri, ss.at[4], rs.at[4], at(ROW if forward else -ROW)).start()

    def spread(ta, ro, ri, po, pc, ss, rs, forward):
        remote(ro, ri, ss.at[4], rs.at[4], at(ROW if forward else -ROW)).wait_recv()
        gate_in_row = first_chip if forward else last_row
        for i in range(2):
            state = ri[i].astype(F32) * gate_in_row
            for c in range(4) if forward else range(3, -1, -1):
                po[2 * c + i] = state.astype(BF16)
                state = ta[2 * c + i].astype(F32) + kappa[c] * state
        for i in range(2):
            pc[2 * y + i] = po[2 * y + i]
        for dy in range(1, 4):
            a2a(po, pc, ss, rs, 5, dy, True).start()

    def finish_start(x, xp, po, pc, sx, res, ss, rs, r_other, r_state, s_own, s_state):
        for dy in range(1, 4):
            a2a(po, pc, ss, rs, 5, dy, False).wait_recv()
        base = core * 8
        for i in range(8):
            state = pc[i].astype(F32)
            sx[i] = (x[base + i].astype(F32) * s_own + state * s_state).astype(BF16)
        final(sx, res, ss, rs).start()
        for i in range(8):
            state = pc[i].astype(F32)
            res[base + i] = (xp[i].astype(F32) * r_other + state * r_state).astype(BF16)

    def final(sx, res, ss, rs, sending=True):
        base = pl.multiple_of((core if sending else 1 - core) * 8, 8)
        return remote(sx, res.at[pl.ds(base, 8)], ss.at[8], rs.at[8], at(1 - 2 * core))

    f_pair.wait_recv()
    combine(fx, fxp, ftc, fta, f_ss, f_rs, is_late + is_early * m_in, is_early + is_late * m_in)
    bulk("f1")
    loads[6].wait()
    loads[7].wait()
    scaling = DIM ** -0.5
    scale2 = scaling * math.log2(math.e)

    def local(h, carry):
        q = q_s[:, columns(h)]
        k = k_s[:, columns(h)]
        v = v_s[:, columns(h)]
        keys, values = kvp[h, 0], kvp[h, 1]
        ga = (g_s[:, columns(h)].astype(F32) * (1.0 - gt[h])).astype(BF16)
        s0 = dot_nt(keys, q) * scale2 + bias[0]
        s1 = dot_nt(k, q) * scale2 + bias[1]
        top = jnp.max(jnp.maximum(s0, s1), axis=0, keepdims=True)
        e0 = jnp.exp2(s0 - top)
        e1 = jnp.exp2(s1 - top)
        inverse = 1.0 / jnp.sum(e0 + e1, axis=0, keepdims=True)
        w0 = e0 * inverse
        w1 = e1 * inverse
        gw0 = dot_nt(values, ga)
        gw1 = dot_nt(v, ga)
        delta = jnp.sum(w0 * gw0 + w1 * gw1, axis=0, keepdims=True)
        ds0 = (w0 * (gw0 - delta) * scaling).astype(BF16)
        ds1 = (w1 * (gw1 - delta) * scaling).astype(BF16)
        wb0 = w0.astype(BF16)
        wb1 = w1.astype(BF16)
        dks[h] = dot_nn(ds0, q).astype(BF16)
        dvs[h] = dot_nn(wb0, ga).astype(BF16)
        out = dot_tn(wb0, values) + dot_tn(wb1, v)
        ol[h] = out
        gate = gt[h]
        rows = jnp.sum(g_s[:, columns(h)].astype(F32) * out, axis=0, keepdims=True)
        gg[h] = rows * (gate * (gate - 1.0))
        dql[h] = dot_tn(ds0, keys) + dot_tn(ds1, k)
        dkl[h] = dot_nn(ds1, q)
        dvl[h] = dot_nn(wb1, ga)
        return carry

    def arrived(h):
        arrival(kvp.at[h], kv_rs.at[h])

    def local_heads(low):
        for h in range(low, low + 2):
            arrived(h)
        lax.fori_loop(low, low + 2, local, 0, unroll=UNROLL)
        bulk(f"l{low}")

    await_ids(False)
    kappa, m_before = far_masks()
    told(0)
    tell(1)

    arrival(zr, z_rs)
    total = jnp.zeros((HEADS, 1, DIM), F32)
    for d in range(1, REACH + 1):
        weight = same(-d, -1) * (me >= d).astype(F32)
        total = total + zr[d - 1] * weight
    zb[...] = total

    def state_part(h, carry):
        lifted = (feature(q_s[:, columns(h)].astype(F32)) * um[...]).astype(BF16)
        fq[h] = lifted
        totals = jnp.broadcast_to(zb[h], (DIM, DIM)).astype(BF16)
        den = dot_nt(lifted, totals)
        inverse = 1.0 / jnp.maximum(den, 1.0)
        inv_s[h] = inverse
        den_s[h] = den
        scaled = g_s[:, columns(h)].astype(F32) * gt[h] * inverse
        bx[place_of(h)] = dot_tn(lifted, scaled.astype(BF16)).astype(BF16)
        return carry

    for i in range(4):
        lax.fori_loop(4 * i, 4 * i + 4, state_part, 0, unroll=4)
        bulk(f"s{i}")
    b_pair = pair_send(bx, bxp, b_ss, b_rs)
    b_pair.start()

    def add_rows(h, rows):
        gg[h] = gg[h] + rows * (1.0 - gt[h])

    ring_out(fta, fro, fri, ftc, f_ss, f_rs, True)
    local_heads(0)
    b_pair.wait_recv()
    combine(bx, bxp, btc, bta, b_ss, b_rs, is_early + is_late * m_before, is_late + is_early * m_before)
    bulk("b1")
    local_heads(2)
    told(1)
    tell(2)
    local_heads(4)
    spread(fta, fro, fri, fpo, fpc, f_ss, f_rs, True)
    bulk("f2")
    local_heads(6)
    local_heads(8)
    ring_out(bta, bro, bri, btc, b_ss, b_rs, False)
    local_heads(10)
    local_heads(12)
    spread(bta, bro, bri, bpo, bpc, b_ss, b_rs, False)
    bulk("b2")
    local_heads(14)

    for i in range(2):
        rows = jnp.zeros((1, DIM), F32)
        for c in range(4):
            product = bta[2 * c + i].astype(F32) * fpo[2 * c + i].astype(F32)
            rows = rows + jnp.sum(product, axis=0, keepdims=True)
        add_rows(2 * spot + i, rows)
    late_core = core == 1
    for i in range(8):
        grads = jnp.where(late_core, bx[core * 8 + i], bxp[i]).astype(F32)
        states = jnp.where(late_core, fxp[i], fx[core * 8 + i]).astype(F32)
        rows = jnp.sum(grads * states, axis=0, keepdims=True)
        add_rows(4 * (i // 2) + 2 * core + i % 2, rows)

    lane = lax.broadcasted_iota(jnp.int32, (1, DIM), 1)
    mine = jnp.zeros((1, DIM), F32)
    for h in range(HEADS):
        mine = mine + jnp.where(lane == h, jnp.sum(gg[h], axis=1, keepdims=True), 0.0)
    red_s[0] = mine

    n_rows = n_ctx // ROW

    def x_copy(d):
        i = d - 1
        return remote(red_s.at[0], red_r.at[i], sent.at[5], red_rs.at[0], at(ROW * d))

    def z_copy(d):
        j = n_rows - 1 + d - 1
        return remote(red_s.at[1], red_r.at[j], sent.at[6], red_rs.at[1], up(d))

    def row_copy(d):
        to = {"ctx": row * ROW + lax.rem(spot + d, ROW)}
        j = n_rows - 1 + n_dp - 1 + d - 1
        return remote(red_s.at[2], red_r.at[j], sent.at[7], red_rs.at[2], to)

    for d in range(1, n_rows):
        x_copy(d).start()
    finish_start(
        fx, fxp, fpo, fpc, fsx, fres, f_ss, f_rs,
        is_late, is_early + is_late * m_before, is_early, is_late + is_early * m_before,
    )
    told(2)
    arrival(red_r.at[pl.ds(0, n_rows - 1)], red_rs.at[0])
    for d in range(1, n_rows):
        mine = mine + red_r[d - 1]
    red_s[1] = mine
    for d in hops:
        z_copy(d).start()
    final(fsx, fres, f_ss, f_rs, False).wait_recv()

    def reads(h, carry):
        state = fres[place_of(h)]
        lifted = fq[h]
        inverse = inv_s[h]
        gate = gt[h]
        grad = g_s[:, columns(h)].astype(F32)
        out = dot_nn(lifted, state) * inverse
        near_out = ol[h]
        att_o[:, columns(h)] = (gate * out + (1.0 - gate) * near_out).astype(BF16)
        scaled_grad = grad * gate
        den = den_s[h]
        active = jnp.where(den > 1.0, inverse, jnp.where(den == 1.0, 0.5, 0.0))
        dden = -jnp.sum(scaled_grad * out, axis=1, keepdims=True) * active
        back = dot_nt((scaled_grad * inverse).astype(BF16), state) + dden * zb[h]
        wide = lifted.astype(F32)
        dzt[h] = jnp.sum(dden * wide, axis=0, keepdims=True)
        dq_o[:, columns(h)] = (dql[h] + back * jnp.minimum(wide, 1.0)).astype(BF16)
        return carry

    lax.fori_loop(0, HEADS, reads, 0, unroll=4)
    for d in range(1, REACH + 1):
        remote(dzt, dzr.at[d - 1], sent.at[4], dz_rs, at(-d)).start()

    half = HEADS * DIM // 2

    def put(i, which):
        src, dst = ((att_o, att_out), (dq_o, dq_out), (dk_o, dk_out), (dv_o, dv_out))[which]
        part = pl.ds(i * half, half)
        return pltpu.make_async_copy(src.at[:, part], dst.at[:, part], out_sem.at[2 * which + i])

    for i in range(2):
        put(i, 0).start()
        put(i, 1).start()
    finish_start(
        bx, bxp, bpo, bpc, bsx, bres, b_ss, b_rs,
        is_early, is_late + is_early * m_in, is_late, is_early + is_late * m_in,
    )

    arrival(dzr, dz_rs)
    total = jnp.zeros((HEADS, 1, DIM), F32)
    for d in range(1, REACH + 1):
        weight = same(d - 1, 0) * (me + d < n_ctx).astype(F32)
        total = total + dzr[d - 1] * weight
    cz[...] = total

    final(bsx, bres, b_ss, b_rs, False).wait_recv()

    def writes(h, carry):
        carried = bres[place_of(h)]
        lifted = fk[h]
        back = dot_nt(v_s[:, columns(h)], carried) + cz[h]
        mem_key = back * jnp.minimum(lifted.astype(F32), 1.0)
        dk_o[:, columns(h)] = (dkl[h] + dkvn[h, 0].astype(F32) + mem_key).astype(BF16)
        mem_value = dot_nn(lifted, carried)
        dv_o[:, columns(h)] = (dvl[h] + dkvn[h, 1].astype(F32) + mem_value).astype(BF16)
        return carry

    def returned(h, carry):
        arrival(dkvn.at[h], dkv_rs.at[h])
        return carry

    for i in range(2):
        low, high = i * HEADS // 2, (i + 1) * HEADS // 2
        lax.fori_loop(low, high, returned, 0)
        lax.fori_loop(low, high, writes, 0, unroll=4)
        put(i, 2).start()
        put(i, 3).start()
    if hops:
        arrival(red_r.at[pl.ds(n_rows - 1, n_dp - 1)], red_rs.at[1])
    for d in hops:
        mine = mine + red_r[n_rows - 1 + d - 1]
    red_s[2] = mine
    for d in range(1, ROW):
        row_copy(d).start()
    arrival(red_r.at[pl.ds(n_rows + n_dp - 2, ROW - 1)], red_rs.at[2])
    for d in range(1, ROW):
        mine = mine + red_r[n_rows - 1 + n_dp - 1 + d - 1]
    gg_out[...] = mine[:, :HEADS]

    if hops:
        arrival(red_r.at[pl.ds(n_rows - 1, n_dp - 1)], sent.at[6])
    arrival(red_r.at[pl.ds(0, n_rows - 1)], sent.at[5])
    arrival(red_r.at[pl.ds(n_rows + n_dp - 2, ROW - 1)], sent.at[7])
    arrival(idr.at[pl.ds(0, len(id_sends))], sent.at[2])
    arrival(zr, sent.at[3])
    arrival(dzr, sent.at[4])
    for x, xp, tc, ta, ro, ri, po, pc, sx, res, ss, rs, forward in (
        (fx, fxp, ftc, fta, fro, fri, fpo, fpc, fsx, fres, f_ss, f_rs, True),
        (bx, bxp, btc, bta, bro, bri, bpo, bpc, bsx, bres, b_ss, b_rs, False),
    ):
        pair_send(x, xp, ss, rs).wait_send()
        for dy in range(1, 4):
            a2a(tc, ta, ss, rs, 1, dy, True).wait_send()
            a2a(po, pc, ss, rs, 5, dy, True).wait_send()
        remote(ro, ri, ss.at[4], rs.at[4], at(ROW if forward else -ROW)).wait_send()
        final(sx, res, ss, rs).wait_send()

    arrival(kvp, sent.at[0])
    arrival(dkvn, sent.at[1])
    for i in range(2):
        for which in range(4):
            put(i, which).wait()


def write_out(*refs):
    ins, outs, sem = refs[:5], refs[5:10], refs[10]
    copies = [pltpu.make_async_copy(a, b, sem.at[i]) for i, (a, b) in enumerate(zip(ins, outs))]
    for copy in copies:
        copy.start()
    for copy in copies:
        copy.wait()


def on_device(n_ctx, n_dp, queries, key_rows, value_rows, doc_ids, gate_logit, grad_out):
    flat = (SEG, HEADS * DIM)
    blocks = (HEADS, DIM, DIM)
    wide = jax.ShapeDtypeStruct(flat, BF16)
    anywhere = pl.BlockSpec(memory_space=pltpu.HBM)
    vmem = pl.BlockSpec(memory_space=pltpu.VMEM)
    free = pl.BlockSpec(memory_space=pl.ANY)
    half = pltpu.VMEM(blocks, BF16)
    full = pltpu.VMEM(blocks, F32)

    def part(n):
        return pltpu.VMEM((n, DIM, DIM), BF16)

    pair_of = pltpu.VMEM((HEADS, 2, DIM, DIM), BF16)
    lanes = pltpu.VMEM((HEADS, 1, DIM), F32)
    reach = pltpu.VMEM((REACH, HEADS, 1, DIM), F32)
    rows = pltpu.VMEM(flat, BF16)
    n_red = ROW - 1 + n_ctx // ROW - 1 + n_dp - 1
    exchange = [half, part(8), part(8), part(8), part(2), part(2), part(8), part(8), part(8), half]
    dma = pltpu.SemaphoreType.DMA
    scratch = (
        [rows] * 4
        + [pltpu.VMEM((2 * REACH + 1, 1, DIM), jnp.int32)]
        + [pair_of] + [half] * 2 + [full] * 2
        + exchange + exchange
        + [full] * 4 + [half] * 2 + [pair_of] + [rows] * 4
        + [lanes, reach, lanes, lanes, reach, lanes, lanes, lanes]
        + [pltpu.VMEM((2, SEG, SEG), F32), pltpu.VMEM((SEG, SEG), F32), pltpu.VMEM((SEG, DIM), F32)]
        + [pltpu.VMEM((3, 1, DIM), F32), pltpu.VMEM((n_red, 1, DIM), F32)]
        + [dma((8,)), dma((8,)), pltpu.SemaphoreType.REGULAR((3,)), dma((8,)), dma((3,)), dma(()), dma(())]
        + [dma((HEADS,))] * 2
        + [dma((9,))] * 4
        + [dma((3,))]
    )
    shapes = [wide] * 4 + [jax.ShapeDtypeStruct((1, HEADS), F32)]
    results = pl.pallas_call(
        functools.partial(kernel, n_ctx, n_dp),
        out_shape=shapes,
        in_specs=[
            anywhere, anywhere, anywhere, anywhere,
            pl.BlockSpec(memory_space=pltpu.SMEM), anywhere,
        ],
        out_specs=[free] * 4 + [vmem],
        scratch_shapes=scratch,
        compiler_params=pltpu.CompilerParams(
            collective_id=0, has_side_effects=True, vmem_limit_bytes=SCOPED
        ),
    )(
        queries.reshape(flat), key_rows.reshape(flat), value_rows.reshape(flat),
        doc_ids.reshape(1, SEG), gate_logit.reshape(1, HEADS), grad_out.reshape(flat),
    )
    written = pl.pallas_call(
        write_out,
        out_shape=shapes,
        in_specs=[vmem] * 5,
        out_specs=[anywhere] * 5,
        scratch_shapes=[dma((5,))],
        compiler_params=pltpu.CompilerParams(vmem_limit_bytes=2**20),
    )(*results)
    shape = (1,) + flat
    return tuple(r.reshape(shape) for r in written[:4]) + (written[4].reshape(HEADS),)


def solution(mesh):
    tokens = P("dp", "ctx", None)
    return jax.shard_map(
        functools.partial(on_device, mesh.shape["ctx"], mesh.shape["dp"]),
        mesh=mesh,
        in_specs=(tokens, tokens, tokens, P("dp", "ctx"), P(), tokens),
        out_specs=(tokens, tokens, tokens, tokens, P()),
        check_vma=False,
    )
```

```python
import functools
import math

import jax
import jax.numpy as jnp
from jax import lax
from jax.experimental import pallas as pl
from jax.experimental.pallas import tpu as pltpu
from jax.sharding import PartitionSpec as P

SEG = 128
DIM = 128
HEADS = 16
ROW = 8
REACH = 8
UNROLL = 2
KV_AT = {"start": (0, 1), "f1": (2, 3, 4, 5), "s2": (6,), "b1": (7, 8, 9), "l2": (10,), "f2": (11, 12, 13), "l6": (14, 15)}
BACK_AT = {f"l{h}": (h, h + 1) for h in range(0, 16, 2)}
SCOPED = 103 * 2**19
MESH = pl.DeviceIdType.MESH
F32 = jnp.float32
BF16 = jnp.bfloat16


def dot_nn(a, b):
    return lax.dot_general(a, b, (((1,), (0,)), ((), ())), preferred_element_type=F32)


def dot_nt(a, b):
    return lax.dot_general(a, b, (((1,), (1,)), ((), ())), preferred_element_type=F32)


def dot_tn(a, b):
    return lax.dot_general(a, b, (((0,), (0,)), ((), ())), preferred_element_type=F32)


def place_of(h):
    return lax.rem(lax.div(h, 2), 2) * 8 + lax.div(h, 4) * 2 + lax.rem(h, 2)


def columns(h):
    return pl.ds(pl.multiple_of(h * DIM, DIM), DIM)


def feature(x):
    return jnp.where(x > 0, x + 1.0, jnp.exp(jnp.minimum(x, 0.0)))


def kernel(
    n_ctx, n_dp,
    q_in, k_in, v_in, ids_in, gate_in, g_in,
    att_out, dq_out, dk_out, dv_out, gg_out,
    q_s, k_s, v_s, g_s, idr, kvp, fk, fq, inv_s, den_s,
    fx, fxp, ftc, fta, fro, fri, fpo, fpc, fsx, fres,
    bx, bxp, btc, bta, bro, bri, bpo, bpc, bsx, bres,
    ol, dql, dkl, dvl, dks, dvs, dkvn, att_o, dq_o, dk_o, dv_o,
    zt, zr, zb, dzt, dzr, cz, gt, gg, bias, wm, um,
    red_s, red_r,
    load_sem, out_sem, ready, sent, ids_rs, z_rs, dz_rs, kv_rs, dkv_rs,
    f_ss, f_rs, b_ss, b_rs, red_rs,
):
    me = lax.axis_index("ctx")
    mz = lax.axis_index("dp")
    row = lax.div(me, ROW)
    spot = lax.rem(me, ROW)
    y = lax.div(spot, 2)
    core = lax.rem(me, 2)

    def at(offset):
        return {"ctx": lax.rem(me + offset + n_ctx, n_ctx)}

    def up(offset):
        return {"dp": lax.rem(mz + offset + n_dp, n_dp)}

    def remote(src, dst, ss, rs, device):
        return pltpu.make_async_remote_copy(
            src_ref=src, dst_ref=dst, send_sem=ss, recv_sem=rs,
            device_id=device, device_id_type=MESH,
        )

    def arrival(ref, sem):
        pltpu.make_async_copy(ref, ref, sem).wait()

    quarter = HEADS * DIM // 4
    loads = []
    for i in range(4):
        part = pl.ds(i * quarter, quarter)
        loads.append(pltpu.make_async_copy(k_in.at[:, part], k_s.at[:, part], load_sem.at[i]))
    for i, (src, dst) in enumerate(((ids_in, idr.at[REACH]), (v_in, v_s), (q_in, q_s), (g_in, g_s))):
        loads.append(pltpu.make_async_copy(src, dst, load_sem.at[4 + i]))
    for copy in loads[4:5] + loads[:4]:
        copy.start()
    barrier = pltpu.get_barrier_semaphore()
    near = [d for d in range(-REACH, REACH + 1) if d] + [n_ctx // 2]
    far = [1, n_dp - 1] if n_dp > 2 else []
    hops = list(range(1, n_dp)) if far else []
    for d in near:
        pl.semaphore_signal(barrier, inc=1, device_id=at(d), device_id_type=MESH)
    for d in far:
        pl.semaphore_signal(barrier, inc=1, device_id=up(d), device_id_type=MESH)

    loads[5].start()
    for h in range(HEADS):
        logit = jnp.full((1, DIM), gate_in[0, h], F32)
        gt[h] = 1.0 / (1.0 + jnp.exp(-logit))
    loads[4].wait()
    own_ids = idr[REACH]
    own_cols = jnp.broadcast_to(own_ids.astype(F32), (SEG, SEG))
    own_rows = jnp.transpose(own_cols)
    own_last = own_ids[:, SEG - 1 :].astype(F32)
    wm[...] = (own_rows == own_last).astype(F32)
    def lift(h, carry):
        lifted = feature(k_s[:, columns(h)].astype(F32)) * wm[...]
        fk[h] = lifted.astype(BF16)
        zt[h] = jnp.sum(lifted, axis=0, keepdims=True)
        return carry

    for i in range(4):
        loads[i].wait()
        lax.fori_loop(4 * i, 4 * i + 4, lift, 0, unroll=4)
    for copy in loads[6:]:
        copy.start()
    pl.semaphore_wait(barrier, len(near) + len(far))

    id_sends = [d for d in range(-(REACH - 1), REACH + 1) if d]
    for i, d in enumerate(id_sends):
        which = {1: 0, -1: 1}.get(d, 2)
        remote(idr.at[REACH], idr.at[REACH - d], sent.at[2], ids_rs.at[which], at(d)).start()
    for d in range(1, REACH + 1):
        remote(zt, zr.at[d - 1], sent.at[3], z_rs, at(d)).start()
    def tell(i):
        if far:
            for d in (2**i, -(2**i)):
                pl.semaphore_signal(ready.at[i], inc=1, device_id=up(d), device_id_type=MESH)

    def told(i):
        if far:
            pl.semaphore_wait(ready.at[i], 2)

    tell(0)

    def send_kv(h, carry):
        remote(k_s.at[:, columns(h)], kvp.at[h, 0], sent.at[0], kv_rs.at[h], at(1)).start()
        remote(v_s.at[:, columns(h)], kvp.at[h, 1], sent.at[0], kv_rs.at[h], at(1)).start()
        return carry

    def send_back(h, carry):
        remote(dks.at[h], dkvn.at[h, 0], sent.at[1], dkv_rs.at[h], at(-1)).start()
        remote(dvs.at[h], dkvn.at[h, 1], sent.at[1], dkv_rs.at[h], at(-1)).start()
        return carry

    def bulk(where):
        for h in KV_AT.get(where, ()):
            send_kv(h, 0)
        for h in BACK_AT.get(where, ()):
            send_back(h, 0)

    loads[5].wait()
    bulk("start")

    def tails(h, carry):
        fx[place_of(h)] = dot_tn(fk[h], v_s[:, columns(h)]).astype(BF16)
        return carry

    lax.fori_loop(0, HEADS, tails, 0, unroll=4)

    def pair_send(x, xp, ss, rs):
        other = pl.ds(pl.multiple_of((1 - core) * 8, 8), 8)
        return remote(x.at[other], xp, ss.at[0], rs.at[0], at(1 - 2 * core))

    f_pair = pair_send(fx, fxp, f_ss, f_rs)
    f_pair.start()

    def await_ids(near_by):
        if near_by:
            arrival(idr.at[REACH - 1], ids_rs.at[0])
            arrival(idr.at[REACH + 1], ids_rs.at[1])
        else:
            arrival(idr.at[pl.ds(0, len(id_sends) - 2)], ids_rs.at[2])

    await_ids(True)

    def last(offset):
        return idr[REACH + offset][:, SEG - 1 :]

    def same(a, b):
        return (last(a) == last(b)).astype(F32)

    is_late = core.astype(F32)
    is_early = 1.0 - is_late
    not_first = (me > 0).astype(F32)
    first_chip = (row > 0).astype(F32)
    last_row = (row < n_ctx // ROW - 1).astype(F32)
    early, late, before = -core, 1 - core, -1 - core
    m_in = same(early, late)

    def far_masks():
        kappa = []
        for c in range(4):
            value = same(2 * c + 1 - spot, 2 * c - 1 - spot)
            kappa.append(value * first_chip if c == 0 else value)
        return kappa, same(early, before) * (me - core > 0).astype(F32)

    prev_ids = idr[REACH - 1]
    prev_rows = jnp.transpose(jnp.broadcast_to(prev_ids.astype(F32), (SEG, SEG)))
    s_pos = lax.broadcasted_iota(jnp.int32, (SEG, SEG), 0)
    t_pos = lax.broadcasted_iota(jnp.int32, (SEG, SEG), 1)
    cut = jnp.full((SEG, SEG), -1e30, F32)
    open_ = jnp.zeros((SEG, SEG), F32)
    shut = (1.0 - not_first) * -1e30
    bias[0] = jnp.where((s_pos > t_pos) & (prev_rows == own_cols), open_, cut) + shut
    bias[1] = jnp.where((s_pos <= t_pos) & (own_rows == own_cols), open_, cut)
    um[...] = (own_rows == prev_ids[:, SEG - 1 :].astype(F32)).astype(F32) * not_first

    def combine(x, xp, tc, ta, ss, rs, c_own, c_other):
        base = core * 8
        for i in range(8):
            tc[i] = (x[base + i].astype(F32) * c_own + xp[i].astype(F32) * c_other).astype(BF16)
        for i in range(2):
            ta[2 * y + i] = tc[2 * y + i]
        for dy in range(1, 4):
            a2a(tc, ta, ss, rs, 1, dy, True).start()

    def a2a(src, dst, ss, rs, slot, dy, sending):
        to_y = lax.rem(y + dy, 4)
        from_y = y if sending else lax.rem(y - dy + 4, 4)
        index = slot + dy - 1
        return remote(
            src.at[pl.ds(2 * to_y, 2)], dst.at[pl.ds(2 * from_y, 2)],
            ss.at[index], rs.at[index], {"ctx": row * ROW + 2 * to_y + core},
        )

    def ring_out(ta, ro, ri, tc, ss, rs, forward):
        for dy in range(1, 4):
            a2a(tc, ta, ss, rs, 1, dy, False).wait_recv()
        for i in range(2):
            total = None
            for c in range(4) if forward else range(3, -1, -1):
                block = ta[2 * c + i].astype(F32)
                total = block if total is None else block + kappa[c] * total
            ro[i] = total.astype(BF16)
        remote(ro, ri, ss.at[4], rs.at[4], at(ROW if forward else -ROW)).start()

    def spread(ta, ro, ri, po, pc, ss, rs, forward):
        remote(ro, ri, ss.at[4], rs.at[4], at(ROW if forward else -ROW)).wait_recv()
        gate_in_row = first_chip if forward else last_row
        for i in range(2):
            state = ri[i].astype(F32) * gate_in_row
            for c in range(4) if forward else range(3, -1, -1):
                po[2 * c + i] = state.astype(BF16)
                state = ta[2 * c + i].astype(F32) + kappa[c] * state
        for i in range(2):
            pc[2 * y + i] = po[2 * y + i]
        for dy in range(1, 4):
            a2a(po, pc, ss, rs, 5, dy, True).start()

    def finish_start(x, xp, po, pc, sx, res, ss, rs, r_other, r_state, s_own, s_state):
        for dy in range(1, 4):
            a2a(po, pc, ss, rs, 5, dy, False).wait_recv()
        base = core * 8
        for i in range(8):
            state = pc[i].astype(F32)
            sx[i] = (x[base + i].astype(F32) * s_own + state * s_state).astype(BF16)
        final(sx, res, ss, rs).start()
        for i in range(8):
            state = pc[i].astype(F32)
            res[base + i] = (xp[i].astype(F32) * r_other + state * r_state).astype(BF16)

    def final(sx, res, ss, rs, sending=True):
        base = pl.multiple_of((core if sending else 1 - core) * 8, 8)
        return remote(sx, res.at[pl.ds(base, 8)], ss.at[8], rs.at[8], at(1 - 2 * core))

    f_pair.wait_recv()
    combine(fx, fxp, ftc, fta, f_ss, f_rs, is_late + is_early * m_in, is_early + is_late * m_in)
    bulk("f1")
    loads[6].wait()
    loads[7].wait()
    scaling = DIM ** -0.5
    scale2 = scaling * math.log2(math.e)

    def local(h, carry):
        q = q_s[:, columns(h)]
        k = k_s[:, columns(h)]
        v = v_s[:, columns(h)]
        keys, values = kvp[h, 0], kvp[h, 1]
        ga = (g_s[:, columns(h)].astype(F32) * (1.0 - gt[h])).astype(BF16)
        s0 = dot_nt(keys, q) * scale2 + bias[0]
        s1 = dot_nt(k, q) * scale2 + bias[1]
        top = jnp.max(jnp.maximum(s0, s1), axis=0, keepdims=True)
        e0 = jnp.exp2(s0 - top)
        e1 = jnp.exp2(s1 - top)
        inverse = 1.0 / jnp.sum(e0 + e1, axis=0, keepdims=True)
        w0 = e0 * inverse
        w1 = e1 * inverse
        gw0 = dot_nt(values, ga)
        gw1 = dot_nt(v, ga)
        delta = jnp.sum(w0 * gw0 + w1 * gw1, axis=0, keepdims=True)
        ds0 = (w0 * (gw0 - delta) * scaling).astype(BF16)
        ds1 = (w1 * (gw1 - delta) * scaling).astype(BF16)
        wb0 = w0.astype(BF16)
        wb1 = w1.astype(BF16)
        dks[h] = dot_nn(ds0, q).astype(BF16)
        dvs[h] = dot_nn(wb0, ga).astype(BF16)
        out = dot_tn(wb0, values) + dot_tn(wb1, v)
        ol[h] = out
        gate = gt[h]
        rows = jnp.sum(g_s[:, columns(h)].astype(F32) * out, axis=0, keepdims=True)
        gg[h] = rows * (gate * (gate - 1.0))
        dql[h] = dot_tn(ds0, keys) + dot_tn(ds1, k)
        dkl[h] = dot_nn(ds1, q)
        dvl[h] = dot_nn(wb1, ga)
        return carry

    def arrived(h):
        arrival(kvp.at[h], kv_rs.at[h])

    def local_heads(low):
        for h in range(low, low + 2):
            arrived(h)
        lax.fori_loop(low, low + 2, local, 0, unroll=UNROLL)
        bulk(f"l{low}")

    await_ids(False)
    kappa, m_before = far_masks()
    told(0)
    tell(1)

    arrival(zr, z_rs)
    total = jnp.zeros((HEADS, 1, DIM), F32)
    for d in range(1, REACH + 1):
        weight = same(-d, -1) * (me >= d).astype(F32)
        total = total + zr[d - 1] * weight
    zb[...] = total

    def state_part(h, carry):
        lifted = (feature(q_s[:, columns(h)].astype(F32)) * um[...]).astype(BF16)
        fq[h] = lifted
        totals = jnp.broadcast_to(zb[h], (DIM, DIM)).astype(BF16)
        den = dot_nt(lifted, totals)
        inverse = 1.0 / jnp.maximum(den, 1.0)
        inv_s[h] = inverse
        den_s[h] = den
        scaled = g_s[:, columns(h)].astype(F32) * gt[h] * inverse
        bx[place_of(h)] = dot_tn(lifted, scaled.astype(BF16)).astype(BF16)
        return carry

    for i in range(4):
        lax.fori_loop(4 * i, 4 * i + 4, state_part, 0, unroll=4)
        bulk(f"s{i}")
    b_pair = pair_send(bx, bxp, b_ss, b_rs)
    b_pair.start()

    def add_rows(h, rows):
        gg[h] = gg[h] + rows * (1.0 - gt[h])

    ring_out(fta, fro, fri, ftc, f_ss, f_rs, True)
    local_heads(0)
    b_pair.wait_recv()
    combine(bx, bxp, btc, bta, b_ss, b_rs, is_early + is_late * m_before, is_late + is_early * m_before)
    bulk("b1")
    local_heads(2)
    told(1)
    tell(2)
    local_heads(4)
    spread(fta, fro, fri, fpo, fpc, f_ss, f_rs, True)
    bulk("f2")
    local_heads(6)
    local_heads(8)
    ring_out(bta, bro, bri, btc, b_ss, b_rs, False)
    finish_start(
        fx, fxp, fpo, fpc, fsx, fres, f_ss, f_rs,
        is_late, is_early + is_late * m_before, is_early, is_late + is_early * m_before,
    )
    local_heads(10)
    local_heads(12)
    spread(bta, bro, bri, bpo, bpc, b_ss, b_rs, False)
    bulk("b2")
    local_heads(14)

    for i in range(2):
        rows = jnp.zeros((1, DIM), F32)
        for c in range(4):
            product = bta[2 * c + i].astype(F32) * fpo[2 * c + i].astype(F32)
            rows = rows + jnp.sum(product, axis=0, keepdims=True)
        add_rows(2 * spot + i, rows)
    late_core = core == 1
    for i in range(8):
        grads = jnp.where(late_core, bx[core * 8 + i], bxp[i]).astype(F32)
        states = jnp.where(late_core, fxp[i], fx[core * 8 + i]).astype(F32)
        rows = jnp.sum(grads * states, axis=0, keepdims=True)
        add_rows(4 * (i // 2) + 2 * core + i % 2, rows)

    lane = lax.broadcasted_iota(jnp.int32, (1, DIM), 1)
    mine = jnp.zeros((1, DIM), F32)
    for h in range(HEADS):
        mine = mine + jnp.where(lane == h, jnp.sum(gg[h], axis=1, keepdims=True), 0.0)
    red_s[0] = mine

    n_rows = n_ctx // ROW

    def x_copy(d):
        i = d - 1
        return remote(red_s.at[0], red_r.at[i], sent.at[5], red_rs.at[0], at(ROW * d))

    def z_copy(d):
        j = n_rows - 1 + d - 1
        return remote(red_s.at[1], red_r.at[j], sent.at[6], red_rs.at[1], up(d))

    def row_copy(d):
        to = {"ctx": row * ROW + lax.rem(spot + d, ROW)}
        j = n_rows - 1 + n_dp - 1 + d - 1
        return remote(red_s.at[2], red_r.at[j], sent.at[7], red_rs.at[2], to)

    for d in range(1, n_rows):
        x_copy(d).start()
    told(2)
    final(fsx, fres, f_ss, f_rs, False).wait_recv()

    def reads(h, carry):
        state = fres[place_of(h)]
        lifted = fq[h]
        inverse = inv_s[h]
        gate = gt[h]
        grad = g_s[:, columns(h)].astype(F32)
        out = dot_nn(lifted, state) * inverse
        near_out = ol[h]
        att_o[:, columns(h)] = (gate * out + (1.0 - gate) * near_out).astype(BF16)
        scaled_grad = grad * gate
        den = den_s[h]
        active = jnp.where(den > 1.0, inverse, jnp.where(den == 1.0, 0.5, 0.0))
        dden = -jnp.sum(scaled_grad * out, axis=1, keepdims=True) * active
        back = dot_nt((scaled_grad * inverse).astype(BF16), state) + dden * zb[h]
        wide = lifted.astype(F32)
        dzt[h] = jnp.sum(dden * wide, axis=0, keepdims=True)
        dq_o[:, columns(h)] = (dql[h] + back * jnp.minimum(wide, 1.0)).astype(BF16)
        return carry

    lax.fori_loop(0, HEADS, reads, 0, unroll=4)
    for d in range(1, REACH + 1):
        remote(dzt, dzr.at[d - 1], sent.at[4], dz_rs, at(-d)).start()

    arrival(red_r.at[pl.ds(0, n_rows - 1)], red_rs.at[0])
    for d in range(1, n_rows):
        mine = mine + red_r[d - 1]
    red_s[1] = mine
    for d in hops:
        z_copy(d).start()
    half = HEADS * DIM // 2

    def put(i, which):
        src, dst = ((att_o, att_out), (dq_o, dq_out), (dk_o, dk_out), (dv_o, dv_out))[which]
        part = pl.ds(i * half, half)
        return pltpu.make_async_copy(src.at[:, part], dst.at[:, part], out_sem.at[2 * which + i])

    for i in range(2):
        put(i, 0).start()
        put(i, 1).start()
    finish_start(
        bx, bxp, bpo, bpc, bsx, bres, b_ss, b_rs,
        is_early, is_late + is_early * m_in, is_late, is_early + is_late * m_in,
    )

    arrival(dzr, dz_rs)
    total = jnp.zeros((HEADS, 1, DIM), F32)
    for d in range(1, REACH + 1):
        weight = same(d - 1, 0) * (me + d < n_ctx).astype(F32)
        total = total + dzr[d - 1] * weight
    cz[...] = total

    final(bsx, bres, b_ss, b_rs, False).wait_recv()

    def writes(h, carry):
        carried = bres[place_of(h)]
        lifted = fk[h]
        back = dot_nt(v_s[:, columns(h)], carried) + cz[h]
        mem_key = back * jnp.minimum(lifted.astype(F32), 1.0)
        dk_o[:, columns(h)] = (dkl[h] + dkvn[h, 0].astype(F32) + mem_key).astype(BF16)
        mem_value = dot_nn(lifted, carried)
        dv_o[:, columns(h)] = (dvl[h] + dkvn[h, 1].astype(F32) + mem_value).astype(BF16)
        return carry

    def returned(h, carry):
        arrival(dkvn.at[h], dkv_rs.at[h])
        return carry

    for i in range(2):
        low, high = i * HEADS // 2, (i + 1) * HEADS // 2
        lax.fori_loop(low, high, returned, 0)
        lax.fori_loop(low, high, writes, 0, unroll=4)
        put(i, 2).start()
        put(i, 3).start()
    if hops:
        arrival(red_r.at[pl.ds(n_rows - 1, n_dp - 1)], red_rs.at[1])
    for d in hops:
        mine = mine + red_r[n_rows - 1 + d - 1]
    red_s[2] = mine
    for d in range(1, ROW):
        row_copy(d).start()
    arrival(red_r.at[pl.ds(n_rows + n_dp - 2, ROW - 1)], red_rs.at[2])
    for d in range(1, ROW):
        mine = mine + red_r[n_rows - 1 + n_dp - 1 + d - 1]
    gg_out[...] = mine[:, :HEADS]

    if hops:
        arrival(red_r.at[pl.ds(n_rows - 1, n_dp - 1)], sent.at[6])
    arrival(red_r.at[pl.ds(0, n_rows - 1)], sent.at[5])
    arrival(red_r.at[pl.ds(n_rows + n_dp - 2, ROW - 1)], sent.at[7])
    arrival(idr.at[pl.ds(0, len(id_sends))], sent.at[2])
    arrival(zr, sent.at[3])
    arrival(dzr, sent.at[4])
    for x, xp, tc, ta, ro, ri, po, pc, sx, res, ss, rs, forward in (
        (fx, fxp, ftc, fta, fro, fri, fpo, fpc, fsx, fres, f_ss, f_rs, True),
        (bx, bxp, btc, bta, bro, bri, bpo, bpc, bsx, bres, b_ss, b_rs, False),
    ):
        pair_send(x, xp, ss, rs).wait_send()
        for dy in range(1, 4):
            a2a(tc, ta, ss, rs, 1, dy, True).wait_send()
            a2a(po, pc, ss, rs, 5, dy, True).wait_send()
        remote(ro, ri, ss.at[4], rs.at[4], at(ROW if forward else -ROW)).wait_send()
        final(sx, res, ss, rs).wait_send()

    arrival(kvp, sent.at[0])
    arrival(dkvn, sent.at[1])
    for i in range(2):
        for which in range(4):
            put(i, which).wait()


def write_out(*refs):
    ins, outs, sem = refs[:5], refs[5:10], refs[10]
    copies = [pltpu.make_async_copy(a, b, sem.at[i]) for i, (a, b) in enumerate(zip(ins, outs))]
    for copy in copies:
        copy.start()
    for copy in copies:
        copy.wait()


def on_device(n_ctx, n_dp, queries, key_rows, value_rows, doc_ids, gate_logit, grad_out):
    flat = (SEG, HEADS * DIM)
    blocks = (HEADS, DIM, DIM)
    wide = jax.ShapeDtypeStruct(flat, BF16)
    anywhere = pl.BlockSpec(memory_space=pltpu.HBM)
    vmem = pl.BlockSpec(memory_space=pltpu.VMEM)
    free = pl.BlockSpec(memory_space=pl.ANY)
    half = pltpu.VMEM(blocks, BF16)
    full = pltpu.VMEM(blocks, F32)

    def part(n):
        return pltpu.VMEM((n, DIM, DIM), BF16)

    pair_of = pltpu.VMEM((HEADS, 2, DIM, DIM), BF16)
    lanes = pltpu.VMEM((HEADS, 1, DIM), F32)
    reach = pltpu.VMEM((REACH, HEADS, 1, DIM), F32)
    rows = pltpu.VMEM(flat, BF16)
    n_red = ROW - 1 + n_ctx // ROW - 1 + n_dp - 1
    exchange = [half, part(8), part(8), part(8), part(2), part(2), part(8), part(8), part(8), half]
    dma = pltpu.SemaphoreType.DMA
    scratch = (
        [rows] * 4
        + [pltpu.VMEM((2 * REACH + 1, 1, DIM), jnp.int32)]
        + [pair_of] + [half] * 2 + [full] * 2
        + exchange + exchange
        + [full] * 4 + [half] * 2 + [pair_of] + [rows] * 4
        + [lanes, reach, lanes, lanes, reach, lanes, lanes, lanes]
        + [pltpu.VMEM((2, SEG, SEG), F32), pltpu.VMEM((SEG, SEG), F32), pltpu.VMEM((SEG, DIM), F32)]
        + [pltpu.VMEM((3, 1, DIM), F32), pltpu.VMEM((n_red, 1, DIM), F32)]
        + [dma((8,)), dma((8,)), pltpu.SemaphoreType.REGULAR((3,)), dma((8,)), dma((3,)), dma(()), dma(())]
        + [dma((HEADS,))] * 2
        + [dma((9,))] * 4
        + [dma((3,))]
    )
    shapes = [wide] * 4 + [jax.ShapeDtypeStruct((1, HEADS), F32)]
    results = pl.pallas_call(
        functools.partial(kernel, n_ctx, n_dp),
        out_shape=shapes,
        in_specs=[
            anywhere, anywhere, anywhere, anywhere,
            pl.BlockSpec(memory_space=pltpu.SMEM), anywhere,
        ],
        out_specs=[free] * 4 + [vmem],
        scratch_shapes=scratch,
        compiler_params=pltpu.CompilerParams(
            collective_id=0, has_side_effects=True, vmem_limit_bytes=SCOPED
        ),
    )(
        queries.reshape(flat), key_rows.reshape(flat), value_rows.reshape(flat),
        doc_ids.reshape(1, SEG), gate_logit.reshape(1, HEADS), grad_out.reshape(flat),
    )
    written = pl.pallas_call(
        write_out,
        out_shape=shapes,
        in_specs=[vmem] * 5,
        out_specs=[anywhere] * 5,
        scratch_shapes=[dma((5,))],
        compiler_params=pltpu.CompilerParams(vmem_limit_bytes=2**20),
    )(*results)
    shape = (1,) + flat
    return tuple(r.reshape(shape) for r in written[:4]) + (written[4].reshape(HEADS),)


def solution(mesh):
    tokens = P("dp", "ctx", None)
    return jax.shard_map(
        functools.partial(on_device, mesh.shape["ctx"], mesh.shape["dp"]),
        mesh=mesh,
        in_specs=(tokens, tokens, tokens, P("dp", "ctx"), P(), tokens),
        out_specs=(tokens, tokens, tokens, tokens, P()),
        check_vma=False,
    )
```
